256 devices in a mesh: rows: 64 (over x, y, z_hi), sub: 4 (over z_lo, core).
Axes of the slice: x: 4, y: 4, z: 8 (z_hi: 4, z_lo: 2; z = z_hi * 2 + z_lo), core: 2. Of those that a mesh axis runs over, the one named last changes fastest.
Arguments:
- right_sides: float32 [262144, 512], P(('rows', 'sub')), may hold values from -6 to 6
- bases_u: float32 [4, 262144, 256], P(None, ('rows', 'sub')), may hold values from -0.375 to 0.375
- bases_v: float32 [4, 262144, 256], P(None, ('rows', 'sub')), may hold values from -0.015625 to 0.015625
- couple_first: float32 [512, 512], P(('rows', 'sub')), may hold values from -0.25 to 0.25
- couple_second: float32 [1024, 512], P(('rows', 'sub')), may hold values from -0.25 to 0.25
- couple_third: float32 [2048, 512], P(('rows', 'sub')), may hold values from -0.25 to 0.25
- couple_fourth: float32 [4096, 512], P(('rows', 'sub')), may hold values from -0.25 to 0.25
Outputs:
- solved: float32 [262144, 512], P(('rows', 'sub'))
The draws below stay inside these ranges and needn't reach their ends.
All inputs are finite; a program needn't handle non-finite values.
Results may differ from the reference program's by a relative error of at most 0.00013.
Values sent between devices are 32-bit elements; how exact they have to be, the bound alone decides.
A program may use at most 64 MiB of HBM per device.

```python
import jax
import jax.numpy as jnp
from jax import lax

RANK = 256
SIDES = 512
LEVELS = 4
ORDER = 262144


def block_levels(own_key, extent, pieces, smallest, largest):
    loudness, own = 1.0, jax.random.fold_in(own_key, 6)
    for dim, shards_of in pieces:
        heights = jnp.exp(jax.random.uniform(jax.random.fold_in(own, dim), (shards_of,), jnp.float32, smallest / len(pieces), largest / len(pieces)))
        loudness = loudness * jnp.repeat(heights, extent[dim] // shards_of).reshape([-1 if axis == dim else 1 for axis in range(len(extent))])
    return loudness


def gaussian(stream_key, extent, spread, most, split=(), kind=jnp.bfloat16):
    level = block_levels(stream_key, extent, split, -0.22, 0.18) if split else 1.0
    drawn = jax.random.normal(stream_key, extent, jnp.float32) * spread * level
    return jnp.minimum(jnp.maximum(drawn, -most), most).astype(kind)


def setup_inputs(seed: int = 0) -> dict:
    arg_keys = jax.random.split(jax.random.key(seed), 8)
    right_sides = gaussian(arg_keys[0], (ORDER, SIDES), 1.0, 6.0, ((0, 256),), jnp.float32)
    bases_u = gaussian(arg_keys[1], (LEVELS, ORDER, RANK), RANK ** -0.5, 0.375, ((1, 256),), jnp.float32)
    bases_v = gaussian(arg_keys[2], (LEVELS, ORDER, RANK), (ORDER // 2) ** -0.5, 0.015625, ((1, 256),), jnp.float32)
    couple_first = gaussian(arg_keys[3], (2 * RANK, 2 * RANK), (2 * RANK) ** -0.5, 0.25, ((0, 256),), jnp.float32)
    couple_second = gaussian(arg_keys[4], (4 * RANK, 2 * RANK), (2 * RANK) ** -0.5, 0.25, ((0, 256),), jnp.float32)
    couple_third = gaussian(arg_keys[5], (8 * RANK, 2 * RANK), (2 * RANK) ** -0.5, 0.25, ((0, 256),), jnp.float32)
    couple_fourth = gaussian(arg_keys[6], (16 * RANK, 2 * RANK), (2 * RANK) ** -0.5, 0.25, ((0, 256),), jnp.float32)
    return {"right_sides": right_sides, "bases_u": bases_u, "bases_v": bases_v, "couple_first": couple_first, "couple_second": couple_second, "couple_third": couple_third, "couple_fourth": couple_fourth}


def reference(right_sides, bases_u, bases_v, couple_first, couple_second, couple_third, couple_fourth):
    couples = (couple_first, couple_second, couple_third, couple_fourth)
    solved = right_sides
    for depth_index in range(LEVELS):
        nodes = 2 ** depth_index
        child_rows = ORDER // (2 * nodes)
        blocks = solved.reshape(2 * nodes, child_rows, SIDES)
        right_blocks = bases_v[depth_index].reshape(2 * nodes, child_rows, RANK)
        sums = jnp.einsum("cnr,cnk->crk", right_blocks, blocks, precision=lax.Precision.HIGHEST)
        paired = sums.reshape(nodes, 2 * RANK, SIDES)
        inverses = couples[depth_index].reshape(nodes, 2 * RANK, 2 * RANK)
        factors = jnp.einsum("nij,njk->nik", inverses, paired, precision=lax.Precision.HIGHEST)
        factors = factors.reshape(2 * nodes, RANK, SIDES)
        left_blocks = bases_u[depth_index].reshape(2 * nodes, child_rows, RANK)
        update = jnp.einsum("cnr,crk->cnk", left_blocks, factors, precision=lax.Precision.HIGHEST)
        solved = solved - update.reshape(ORDER, SIDES)
    return solved
```

```python
import functools

import jax
import jax.numpy as jnp
from jax import lax
from jax.experimental import pallas as pl
from jax.experimental.pallas import tpu as pltpu
from jax.sharding import PartitionSpec as P

F32 = jnp.float32
BF16 = jnp.bfloat16
MESH = pl.DeviceIdType.MESH

RANK = 256
SIDES = 512
SHARE = 32
ROWS = 1024
STREAMS = (
    ((0, 0), (256, 0)),
    ((0, 1), (256, 1)),
    ((512, 1), (512, 2)),
    ((0, 2), (256, 2)),
    ((768, 2), (512, 3)),
    ((0, 3), (256, 3)),
    ((768, 3), (1024, 3)),
)
NS = len(STREAMS)
KROWS = (8, 16, 32, 64)
KLINES = (8, 4, 2, 1)
KOFF = (0, 8, 24, 56)


def split(value):
    high = value.astype(BF16)
    return high, (value - high.astype(F32)).astype(BF16)


def product(left, right, dims):
    def one(a, b):
        return lax.dot_general(a, b, (dims, ((), ())), preferred_element_type=F32)

    return one(left[0], right[0]) + (one(left[0], right[1]) + one(left[1], right[0]))


NN = ((1,), (0,))
NT = ((1,), (1,))


def solve_kernel(
    rhs_hbm, u_hbm, v_hbm, k_own, f_out,
    rhs_in, u_in, v_in, a_hi, a_lo, v_hi, v_lo, part,
    cb, rp, rm, share, yb, y1b, xb, xs, wfull, ffull, sibs, sib,
    kz, k0, k1, k2, k3, kflat,
    in_sem, out_sem,
    core_s, core_r, zp_s, zp_r, zm_s, zm_r, y_s, y_r, y1_s, y1_r, x_s, x_r, sib_s, sib_r,
    agp_s, agp_r, agm_s, agm_r, agc_s, agc_r,
    kp_s, kp_r, km_s, km_r, kf_s, kf_r, kc_s, kc_r,
):
    row_index = lax.axis_index("rows")
    sub_index = lax.axis_index("sub")
    x = row_index // 16
    y = row_index // 4 % 4
    z = row_index % 4 * 2 + sub_index // 2
    c = sub_index % 2

    def device(x, y, z, c):
        return (x * 16 + y * 4 + z // 2, z % 2 * 2 + c)

    partner = device(x, y, z, 1 - c)
    up = device(x, y, (z + 1) % 8, c)
    down = device(x, y, (z + 7) % 8, c)
    y_peer = [device(x, (y + d) % 4, z, c) for d in (1, 2, 3)]
    x_peer = [device((x + d) % 4, y, z, c) for d in (1, 2, 3)]
    y_odd, x_odd = y % 2, x % 2
    y_pair = device(x, y + 1 - 2 * y_odd, z, c)
    x_pair = device(x + 1 - 2 * x_odd, y, z, c)
    y_far = device(x, 3 - y, z, c)

    sent = []

    def send(src, dst, s, r, to):
        copy = pltpu.make_async_remote_copy(
            src_ref=src, dst_ref=dst, send_sem=s, recv_sem=r, device_id=to, device_id_type=MESH
        )
        copy.start()
        sent.append(copy)
        return copy

    loads = {}

    def load(name, src, dst, index):
        copy = pltpu.make_async_copy(src, dst, in_sem.at[index])
        copy.start()
        loads[name] = copy

    load("rhs", rhs_hbm, rhs_in, 0)
    load("v0", v_hbm.at[0], v_in.at[0], 1)
    load("v1", v_hbm.at[1], v_in.at[1], 2)
    load("u0", u_hbm.at[0], u_in.at[0], 3)
    load("v2", v_hbm.at[2], v_in.at[2], 4)
    load("u1", u_hbm.at[1], u_in.at[1], 5)
    load("v3", v_hbm.at[3], v_in.at[3], 6)
    load("u2", u_hbm.at[2], u_in.at[2], 7)

    barrier = pltpu.get_barrier_semaphore()
    peers = [partner, up, down] + y_peer + x_peer
    for peer in peers:
        pl.semaphore_signal(barrier, inc=1, device_id=peer, device_id_type=MESH)
    pl.semaphore_wait(barrier, len(peers))

    def at(place):
        return pl.ds(pl.multiple_of(place % 8 * SHARE, SHARE), SHARE)

    half = pl.ds(pl.multiple_of(c * RANK, RANK), RANK)
    other = pl.ds(pl.multiple_of((1 - c) * RANK, RANK), RANK)

    kasm = (k0, k1, k2, k3)
    kline = (x_odd * 4 + y, y, y_odd, 0)
    kc = {}

    def k_piece(origin):
        return kz.at[origin % 8]

    def k_start():
        kz[z] = k_own[...]
        kc["p", 1] = send(k_piece(z), k_piece(z), kp_s.at[0], kp_r.at[0], up)
        kc["m", 1] = send(k_piece(z), k_piece(z), km_s.at[0], km_r.at[0], down)

    def k_step(k):
        kc["p", k - 1].wait_recv()
        came = k_piece(z + 9 - k)
        kc["p", k] = send(came, came, kp_s.at[k - 1], kp_r.at[k - 1], up)
        kc["m", k - 1].wait_recv()
        if k <= 3:
            came = k_piece(z + k - 1)
            kc["m", k] = send(came, came, km_s.at[k - 1], km_r.at[k - 1], down)

    def k_lines():
        kc["p", 4].wait_recv()
        for level in range(4):
            kasm[level][kline[level], :, c] = kz[:, KOFF[level]:KOFF[level] + KROWS[level]]
        for d in range(3):
            kc["y0", d] = send(
                kz.at[:, 0:8], k0.at[kline[0], :, c], kf_s.at[d], kf_r.at[d], y_peer[d]
            )
            kc["y1", d] = send(
                kz.at[:, 8:24], k1.at[kline[1], :, c], kf_s.at[3 + d], kf_r.at[3 + d], y_peer[d]
            )
        kc["y2"] = send(kz.at[:, 24:56], k2.at[kline[2], :, c], kf_s.at[6], kf_r.at[6], y_pair)
        kc["c", 3] = send(k3.at[:, :, c], k3.at[:, :, c], kc_s.at[3], kc_r.at[3], partner)

    def k_far():
        for d in range(3):
            kc["y0", d].wait_recv()
        lines = pl.ds(x_odd * 4, 4)
        kc["x"] = send(
            k0.at[lines, :, c], k0.at[lines, :, c], kf_s.at[7], kf_r.at[7], x_pair
        )
        for d in range(3):
            kc["y1", d].wait_recv()
        kc["y2"].wait_recv()
        for level in (1, 2):
            kc["c", level] = send(
                kasm[level].at[:, :, c], kasm[level].at[:, :, c],
                kc_s.at[level], kc_r.at[level], partner,
            )

    def k_core():
        kc["x"].wait_recv()
        kc["c", 0] = send(k0.at[:, :, c], k0.at[:, :, c], kc_s.at[0], kc_r.at[0], partner)

    def k_matrix(level):
        kc["c", level].wait_recv()
        kflat[...] = kasm[level][...].reshape(4 * RANK, 128)
        return jnp.concatenate([kflat[pl.ds(b, RANK, stride=4), :] for b in range(4)], axis=1)

    def set_a(value, first):
        turned = jnp.transpose(value)
        high, low = split(turned)
        a_hi[first:first + value.shape[1], :] = high
        a_lo[first:first + value.shape[1], :] = low

    def set_v(level):
        loads["v%d" % level].wait()
        high, low = split(v_in[level])
        v_hi[level] = high
        v_lo[level] = low

    def compute(s):
        if s == 0:
            loads["rhs"].wait()
            set_a(rhs_in[...], 0)
            set_v(0)
        if s == 1:
            set_v(1)
        if s == 2:
            loads["u0"].wait()
            set_a(u_in[0], 512)
            set_v(2)
        if s == 4:
            loads["u1"].wait()
            set_a(u_in[1], 768)
            set_v(3)
        if s == 6:
            loads["u2"].wait()
            set_a(u_in[2], 1024)
        for index, (first, level) in enumerate(STREAMS[s]):
            left = (a_hi[first:first + RANK, :], a_lo[first:first + RANK, :])
            part[s, index * RANK:(index + 1) * RANK] = product(left, (v_hi[level], v_lo[level]), NN)

    cp = {}

    def core_send(s):
        cp["c", s] = send(part.at[s, other], cb.at[s], core_s.at[s], core_r.at[s], partner)

    def scatter(s, k):
        if k == 1:
            cp["c", s].wait_recv()
            cb[s] += part[s, half]
            src_p, src_m = cb.at[s, at(z + 4)], cb.at[s, at(z + 5)]
        elif k <= 4:
            cp["p", s, k - 1].wait_recv()
            rp[s, k - 2] += cb[s, at(z + 5 - k)]
            src_p = rp.at[s, k - 2]
        if k <= 4:
            cp["p", s, k] = send(src_p, rp.at[s, k - 1], zp_s.at[s, k - 1], zp_r.at[s, k - 1], up)
        if 2 <= k <= 4:
            cp["m", s, k - 1].wait_recv()
            if k <= 3:
                rm[s, k - 2] += cb[s, at(z + 4 + k)]
                src_m = rm.at[s, k - 2]
        if k <= 3:
            cp["m", s, k] = send(src_m, rm.at[s, k - 1], zm_s.at[s, k - 1], zm_r.at[s, k - 1], down)
        if k == 5:
            cp["p", s, 4].wait_recv()
            share[s] = cb[s, at(z)] + rp[s, 3] + rm[s, 2]
            if s < 3:
                for d in range(3):
                    cp["y", s, d] = send(
                        share.at[s], yb.at[s, d], y_s.at[s, d], y_r.at[s, d], y_peer[d]
                    )
            elif s < 5:
                cp["y1", s] = send(
                    share.at[s], y1b.at[s - 3], y1_s.at[s - 3], y1_r.at[s - 3], y_pair
                )

    def y_wait(s):
        if s < 3:
            for d in range(3):
                cp["y", s, d].wait_recv()
        else:
            cp["y1", s].wait_recv()

    def y_total(s):
        return (share[s] + yb[s, 0]) + (yb[s, 1] + yb[s, 2])

    def full_of(i):
        return wfull.at[i] if i < 3 else ffull.at[i - 3]

    def spot(origin):
        return pl.ds(pl.multiple_of(c * RANK + origin % 8 * SHARE, SHARE), SHARE)

    def gather_start(i, value):
        full = full_of(i)
        full[spot(z), :] = value
        own = full.at[spot(z), :]
        cp["gp", i, 1] = send(own, own, agp_s.at[i, 0], agp_r.at[i, 0], up)
        cp["gm", i, 1] = send(own, own, agm_s.at[i, 0], agm_r.at[i, 0], down)
        cp["gc", i, 0] = send(own, own, agc_s.at[i, 0], agc_r.at[i, 0], partner)

    def gather_step(i, k):
        full = full_of(i)
        cp["gp", i, k - 1].wait_recv()
        came = full.at[spot(z + 9 - k), :]
        if k <= 4:
            cp["gp", i, k] = send(came, came, agp_s.at[i, k - 1], agp_r.at[i, k - 1], up)
        cp["gc", i, k - 1] = send(came, came, agc_s.at[i, k - 1], agc_r.at[i, k - 1], partner)
        if k <= 4:
            cp["gm", i, k - 1].wait_recv()
            came = full.at[spot(z + k - 1), :]
            if k <= 3:
                cp["gm", i, k] = send(came, came, agm_s.at[i, k - 1], agm_r.at[i, k - 1], down)
            cp["gc", i, k + 3] = send(came, came, agc_s.at[i, k + 3], agc_r.at[i, k + 3], partner)

    def gather_end(i):
        for k in range(8):
            cp["gc", i, k].wait_recv()

    def w_block(l, m):
        index, first = {(1, 0): (0, 0), (2, 0): (0, 256), (2, 1): (1, 0), (3, 0): (1, 256),
                        (3, 1): (2, 0), (3, 2): (2, 256)}[l, m]
        return split(wfull[index, first:first + RANK])

    factors = {}
    out_copy = {}

    def pair(own, sibling, upper):
        return jnp.where(
            upper == 0,
            jnp.concatenate([own, sibling], axis=1),
            jnp.concatenate([sibling, own], axis=1),
        )

    def factor(level, paired):
        value = product(split(paired), split(k_matrix(level)), NT)
        factors[level] = split(value)
        gather_start(3 + level, value)

    def level_0():
        for d in range(3):
            cp["x", d].wait_recv()
        even = x_odd == 0
        own = xs[...] + jnp.where(even, xb[2], xb[0])
        sibling = xb[1] + jnp.where(even, xb[0], xb[2])
        factor(0, pair(own, sibling, x // 2))

    def exchange(level, value):
        sibs[level - 1] = value
        to = (x_pair, y_far, y_pair)[level - 1]
        cp["sib", level] = send(
            sibs.at[level - 1], sib.at[level - 1], sib_s.at[level - 1], sib_r.at[level - 1], to
        )

    def level_sums(level):
        value = (y_total(1), share[3] + y1b[0], share[5])[level - 1]
        for m in range(level):
            value = value - product(factors[m], w_block(level, m), NN)
        exchange(level, value)

    def level_factor(level):
        cp["sib", level].wait_recv()
        upper = (x_odd, y // 2, y_odd)[level - 1]
        factor(level, pair(sibs[level - 1], sib[level - 1], upper))

    def to_x():
        y_wait(0)
        xs[...] = y_total(0)
        for d in range(3):
            cp["x", d] = send(xs, xb.at[d], x_s.at[d], x_r.at[d], x_peer[d])

    def w_first():
        y_wait(2)
        near = jnp.where(y_odd == 0, yb[2, 2], yb[2, 0])
        gather_start(0, jnp.where(c == 0, y_total(2), share[2] + near))

    def w_second():
        y_wait(4)
        gather_start(1, jnp.where(c == 0, share[4] + y1b[1], share[4]))

    def w_third():
        gather_start(2, share[6])

    def put(level):
        gather_end(3 + level)
        copy = pltpu.make_async_copy(ffull.at[level], f_out.at[level], out_sem.at[level])
        copy.start()
        out_copy[level] = copy

    extras = {
        0: [k_start],
        1: [functools.partial(k_step, 2)],
        2: [functools.partial(k_step, 3)],
        3: [functools.partial(k_step, 4)],
        4: [k_lines],
        5: [k_far],
        6: [to_x, k_core],
        7: [functools.partial(y_wait, 1)],
        8: [w_first, level_0],
        9: [functools.partial(y_wait, 3)],
        10: [w_second],
        11: [w_third],
        12: [functools.partial(gather_end, 0), functools.partial(level_sums, 1)],
        13: [functools.partial(level_factor, 1)],
        14: [functools.partial(gather_end, 1), functools.partial(level_sums, 2)],
        15: [functools.partial(level_factor, 2)],
        16: [functools.partial(gather_end, 2), functools.partial(level_sums, 3)],
        17: [functools.partial(level_factor, 3), functools.partial(put, 0), functools.partial(put, 1)],
        20: [functools.partial(put, 2)],
        22: [functools.partial(put, 3)],
    }
    starts = {0: 8, 1: 10, 2: 11, 3: 8, 4: 13, 5: 15, 6: 17}
    for t in range(23):
        for s in range(NS):
            if 1 <= t - s <= 5:
                scatter(s, t - s)
        for i in (0, 3, 1, 2, 4, 5, 6):
            if 1 <= t - starts[i] <= 4:
                gather_step(i, t - starts[i] + 1)
        if t == 0:
            k_start()
        else:
            for extra in extras.get(t, []):
                extra()
        if t < NS:
            compute(t)
            core_send(t)
    for level in range(4):
        out_copy[level].wait()
    for copy in sent:
        copy.wait_send()


def solve(rhs, u, v, k_own):
    dma = pltpu.SemaphoreType.DMA
    any_space = pl.BlockSpec(memory_space=pl.ANY)
    pairs = []
    for shape in ((NS,), (NS, 4), (NS, 3), (3, 3), (2,), (3,), (3,), (7, 4), (7, 3), (7, 8), (4,), (3,), (8,), (4,)):
        pairs += [dma(shape), dma(shape)]
    vm = pltpu.VMEM
    return pl.pallas_call(
        solve_kernel,
        out_shape=jax.ShapeDtypeStruct((4, SIDES, RANK), F32),
        in_specs=[any_space, any_space, any_space, pl.BlockSpec(memory_space=pltpu.VMEM)],
        out_specs=any_space,
        scratch_shapes=[
            vm((ROWS, SIDES), F32), vm((3, ROWS, RANK), F32), vm((4, ROWS, RANK), F32),
            vm((1280, ROWS), BF16), vm((1280, ROWS), BF16),
            vm((4, ROWS, RANK), BF16), vm((4, ROWS, RANK), BF16),
            vm((NS, SIDES, RANK), F32),
            vm((NS, RANK, RANK), F32), vm((NS, 4, SHARE, RANK), F32), vm((NS, 3, SHARE, RANK), F32),
            vm((NS, SHARE, RANK), F32), vm((3, 3, SHARE, RANK), F32), vm((2, SHARE, RANK), F32),
            vm((3, SHARE, RANK), F32), vm((SHARE, RANK), F32),
            vm((3, SIDES, RANK), F32), vm((4, SIDES, RANK), F32),
            vm((3, SHARE, RANK), F32), vm((3, SHARE, RANK), F32),
            vm((8, 120, 128), F32),
            vm((8, 8, 2, 8, 128), F32), vm((4, 8, 2, 16, 128), F32),
            vm((2, 8, 2, 32, 128), F32), vm((1, 8, 2, 64, 128), F32),
            vm((4 * RANK, 128), F32),
            dma((8,)), dma((4,)),
        ] + pairs,
        compiler_params=pltpu.CompilerParams(
            collective_id=0, has_side_effects=True, vmem_limit_bytes=60 * 1024 * 1024
        ),
        name="solve",
    )(rhs, u, v, k_own)


def update_kernel(rhs_ref, u_ref, f_ref, out_ref, f_hi, f_lo):
    @pl.when(pl.program_id(0) == 0)
    def _():
        high, low = split(f_ref[...])
        f_hi[...] = high
        f_lo[...] = low

    total = rhs_ref[...]
    for level in range(4):
        total = total - product(split(u_ref[level]), (f_hi[level], f_lo[level]), NT)
    out_ref[...] = total


def update(rhs, u, f):
    block = 256
    return pl.pallas_call(
        update_kernel,
        out_shape=jax.ShapeDtypeStruct((ROWS, SIDES), F32),
        grid=(ROWS // block,),
        in_specs=[
            pl.BlockSpec((block, SIDES), lambda i: (i, 0)),
            pl.BlockSpec((4, block, RANK), lambda i: (0, i, 0)),
            pl.BlockSpec((4, SIDES, RANK), lambda i: (0, 0, 0)),
        ],
        out_specs=pl.BlockSpec((block, SIDES), lambda i: (i, 0)),
        scratch_shapes=[pltpu.VMEM((4, SIDES, RANK), BF16), pltpu.VMEM((4, SIDES, RANK), BF16)],
        compiler_params=pltpu.CompilerParams(vmem_limit_bytes=40 * 1024 * 1024),
        name="update",
    )(rhs, u, f)


def local(right_sides, bases_u, bases_v, couple_first, couple_second, couple_third, couple_fourth):
    k_own = jnp.concatenate(
        [k.reshape(-1, 128) for k in (couple_first, couple_second, couple_third, couple_fourth)], axis=0
    )
    f = solve(right_sides, bases_u, bases_v, k_own)
    return update(right_sides, bases_u, f)


def solution(mesh):
    placed = (
        P(("rows", "sub"), None),
        P(None, ("rows", "sub"), None),
        P(None, ("rows", "sub"), None),
        P(("rows", "sub"), None),
        P(("rows", "sub"), None),
        P(("rows", "sub"), None),
        P(("rows", "sub"), None),
    )
    return jax.shard_map(
        local, mesh=mesh, in_specs=placed, out_specs=P(("rows", "sub"), None), check_vma=False
    )
```

```python
import functools

import jax
import jax.numpy as jnp
from jax import lax
from jax.experimental import pallas as pl
from jax.experimental.pallas import tpu as pltpu
from jax.sharding import PartitionSpec as P

F32 = jnp.float32
BF16 = jnp.bfloat16
MESH = pl.DeviceIdType.MESH

RANK = 256
SIDES = 512
ROWS = 1024
STREAMS = (
    (0, 512, 0, True),
    (512, 256, 1, True),
    (512, 512, 2, True),
    (0, 512, 1, True),
    (0, 512, 2, True),
    (512, 768, 3, False),
    (0, 512, 3, False),
)
G0, W1, W2, G1, G2, W3, G3 = range(7)
NS = len(STREAMS)
QUARTER = tuple(rows // 4 for _, rows, _, _ in STREAMS)
PIECE = tuple(rows // 32 for _, rows, _, _ in STREAMS)
WIDE = tuple(1 if paired else 2 for _, _, _, paired in STREAMS)
GATHERED = (W1, W2, W3)
KROWS = (8, 16, 32, 64)
KOFF = (0, 8, 24)


def split(value):
    high = value.astype(BF16)
    return high, (value - high.astype(F32)).astype(BF16)


def product(left, right, dims):
    def one(a, b):
        return lax.dot_general(a, b, (dims, ((), ())), preferred_element_type=F32)

    return one(left[0], right[0]) + (one(left[0], right[1]) + one(left[1], right[0]))


NN = ((1,), (0,))
NT = ((1,), (1,))


def solve_kernel(*refs):
    refs = list(refs)

    def take(count=None):
        if count is None:
            return refs.pop(0)
        return [refs.pop(0) for _ in range(count)]

    rhs_hbm, u_hbm, v_hbm = take(3)
    k_own = take(4)
    solved = take()
    u_in, v_in, a_hi, a_lo, v_hi, v_lo = take(6)
    part, cb, pb, rz, share, yb = [take(NS) for _ in range(6)]
    xb, xs = take(2)
    wfull = take(3)
    ffull, f_hi, f_lo, sibs, sib = take(5)
    kown, kz, k0, k1, k2, k3, kflat = take(7)
    in_sem = take()
    (core_s, core_r, pair_s, pair_r, z_s, z_r, y_s, y_r, x_s, x_r, sib_s, sib_r,
     gz_s, gz_r, gc_s, gc_r, kz_s, kz_r, kf_s, kf_r, kc_s, kc_r) = take(22)
    assert not refs

    row_index = lax.axis_index("rows")
    sub_index = lax.axis_index("sub")
    x = row_index // 16
    y = row_index // 4 % 4
    z = row_index % 4 * 2 + sub_index // 2
    c = sub_index % 2
    way = 1 - 2 * c

    def line(steps):
        return (z + way * steps + 16) % 8

    def device(x, y, z, c):
        return (x * 16 + y * 4 + z // 2, z % 2 * 2 + c)

    partner = device(x, y, z, 1 - c)
    z_peer = {steps: device(x, y, line(steps), c) for steps in (1, -1, 2, -2)}
    y_peer = [device(x, (y + d) % 4, z, c) for d in (1, 2, 3)]
    x_peer = [device((x + d) % 4, y, z, c) for d in (1, 2, 3)]
    y_odd, x_odd = y % 2, x % 2
    y_pair = device(x, y + 1 - 2 * y_odd, z, c)
    x_pair = device(x + 1 - 2 * x_odd, y, z, c)
    y_far = device(x, 3 - y, z, c)

    def describe(src, dst, s, r, to):
        return pltpu.make_async_remote_copy(
            src_ref=src, dst_ref=dst, send_sem=s, recv_sem=r, device_id=to, device_id_type=MESH
        )

    drains = {}

    def send(src, dst, s, r, to, drain):
        describe(src, dst, s, r, to).start()
        key, ref = drain
        drains[key] = (s, r, ref)

    def arrived(ref, r, s):
        describe(ref, ref, s, r, partner).wait_recv()

    barrier = pltpu.get_barrier_semaphore()
    peers = [partner] + list(z_peer.values()) + y_peer + x_peer
    for peer in peers:
        pl.semaphore_signal(barrier, inc=1, device_id=peer, device_id_type=MESH)

    loads = {}

    def load(name, src, dst, index):
        copy = pltpu.make_async_copy(src, dst, in_sem.at[index])
        copy.start()
        loads[name] = copy

    load("rhs", rhs_hbm, solved, 0)
    load("v0", v_hbm.at[0], v_in.at[0], 1)

    def load_rest():
        order = (("u", 0), ("v", 1), ("u", 1), ("v", 2), ("u", 2), ("v", 3), ("u", 3))
        for index, (name, level) in enumerate(order):
            src, dst = (u_hbm, u_in) if name == "u" else (v_hbm, v_in)
            load("%s%d" % (name, level), src.at[level], dst.at[level], 2 + index)

    kasm = (k0, k1, k2, k3)
    kline = (x_odd * 4 + y, y, y_odd, 0)

    def k_piece(which, origin):
        return kz.at[origin] if which == 0 else k3.at[0, origin, c]

    def k_send(which, index, origin, steps):
        ref = k_piece(which, origin)
        group = (0, 0, 1, 1, 2, 2, 2)[index]
        every = kz.at[0:7] if which == 0 else k3.at[0, 0:7, c]
        send(ref, ref, kz_s.at[which], kz_r.at[which, group], z_peer[steps], (("kz", which), every))

    def k_wait(which, group):
        count = (2, 2, 3)[group]
        ref = kz.at[0:count] if which == 0 else k3.at[0, 0:count, c]
        arrived(ref, kz_r.at[which, group], kz_s.at[which])

    def k_start(which):
        for level in (0, 1, 2) if which == 0 else (3,):
            count = KROWS[level] // 4
            for b in range(4):
                place = pl.ds(KOFF[level] + b if level < 3 else b, count, stride=4)
                kown[which, place, :] = k_own[level][:, b * 128:(b + 1) * 128]
        if which == 0:
            kz[z] = kown[0, 0:56, :]
        else:
            k3[0, z, c] = kown[1]
        for index, steps in enumerate((2, -2, 1, -1)):
            k_send(which, index, z, steps)

    def k_step(which):
        k_wait(which, 0)
        k_send(which, 4, line(-2), 2)
        k_send(which, 5, line(-2), 1)
        k_send(which, 6, line(2), -1)

    def k_end(which):
        k_wait(which, 1)
        k_wait(which, 2)

    def k_core(level):
        ref = kasm[level].at[:, :, c]
        send(ref, ref, kc_s.at[level], kc_r.at[level], partner, (("kc", level), ref))

    def k_lines_first():
        k_end(0)
        for level in range(3):
            kasm[level][kline[level], :, c] = kz[:, KOFF[level]:KOFF[level] + KROWS[level]]
        for d in range(3):
            send(
                kz.at[:, 0:8], k0.at[kline[0], :, c], kf_s.at[0], kf_r.at[0], y_peer[d],
                ("kf0", k0.at[0:3, :, c]),
            )

    def k_lines_more():
        for d in range(3):
            send(
                kz.at[:, 8:24], k1.at[kline[1], :, c], kf_s.at[1], kf_r.at[1], y_peer[d],
                ("kf1", k1.at[0:3, :, c]),
            )
        send(
            kz.at[:, 24:56], k2.at[kline[2], :, c], kf_s.at[2], kf_r.at[2], y_pair,
            ("kf2", k2.at[0, :, c]),
        )

    def k_far():
        arrived(k0.at[0:3, :, c], kf_r.at[0], kf_s.at[0])
        ref = k0.at[pl.ds(x_odd * 4, 4), :, c]
        send(ref, ref, kf_s.at[3], kf_r.at[3], x_pair, ("kf3", ref))

    def k_near():
        arrived(k0.at[0:4, :, c], kf_r.at[3], kf_s.at[3])
        k_core(0)

    def k_middle():
        arrived(k1.at[0:3, :, c], kf_r.at[1], kf_s.at[1])
        k_core(1)
        arrived(k2.at[0, :, c], kf_r.at[2], kf_s.at[2])
        k_core(2)

    def k_last():
        k_end(1)
        k_core(3)

    def k_matrix(level):
        arrived(kasm[level].at[:, :, c], kc_r.at[level], kc_s.at[level])
        kflat[...] = kasm[level][...].reshape(4 * RANK, 128)
        return jnp.concatenate([kflat[pl.ds(b, RANK, stride=4), :] for b in range(4)], axis=1)

    def set_a(value, first):
        turned = jnp.transpose(value)
        high, low = split(turned)
        a_hi[first:first + value.shape[1], :] = high
        a_lo[first:first + value.shape[1], :] = low

    def set_v(level):
        loads["v%d" % level].wait()
        high, low = split(v_in[level])
        v_hi[level] = high
        v_lo[level] = low

    def set_u(level):
        loads["u%d" % level].wait()
        set_a(u_in[level], 512 + RANK * level)

    def compute(s):
        if s == 0:
            loads["rhs"].wait()
            load_rest()
            set_a(solved[...], 0)
            set_v(0)
        elif s == 1:
            set_u(0)
            set_v(1)
        elif s == 2:
            set_u(1)
            set_v(2)
        elif s == 5:
            set_u(2)
            set_v(3)
        first, rows, level, _ = STREAMS[s]
        for index in range(rows // RANK):
            own = slice(first + index * RANK, first + (index + 1) * RANK)
            value = product((a_hi[own, :], a_lo[own, :]), (v_hi[level], v_lo[level]), NN)
            count = min(QUARTER[s], RANK // 4 if rows != 512 else RANK // 2)
            for at in range(0, RANK, count):
                c_at, rest = divmod(index * RANK + at, 2 * QUARTER[s])
                p_at, row = divmod(rest, QUARTER[s])
                part[s][c_at, p_at, row:row + count, :] = value[at:at + count]

    def core_send(s):
        send(part[s].at[1 - c], cb[s], core_s.at[s], core_r.at[s], partner, (("core", s), cb[s]))

    def piece(s, steps):
        lines = pl.ds(y_odd, 1) if WIDE[s] == 1 else pl.ds(0, 2)
        count = PIECE[s]
        return cb[s].at[lines, pl.ds(pl.multiple_of(line(steps) * count, count), count)]

    def z_send(s, src, index, steps):
        group = 0 if index < 3 else 1
        send(src, rz[s].at[index], z_s.at[s], z_r.at[s, group], z_peer[steps], (("z", s), rz[s]))

    def chain_first(s):
        z_send(s, piece(s, 4), 1, 2)
        z_send(s, piece(s, 3), 0, 1)
        z_send(s, piece(s, -3), 2, -1)
        z_send(s, piece(s, 1), 3, 1)
        z_send(s, piece(s, -1), 4, -1)

    def chain_second(s):
        arrived(rz[s].at[0:3], z_r.at[s, 0], z_s.at[s])
        rz[s][0] = (rz[s][0] + rz[s][1]) + piece(s, 2)[...]
        z_send(s, rz[s].at[0], 5, 2)
        rz[s][2] += piece(s, -2)[...]
        z_send(s, rz[s].at[2], 6, -2)

    def finish(s):
        arrived(rz[s].at[3:7], z_r.at[s, 1], z_s.at[s])
        share[s][...] = piece(s, 0)[...] + ((rz[s][3] + rz[s][4]) + (rz[s][5] + rz[s][6]))
        if s in (G0, W1, G1):
            to = y_peer
        elif s in (W2, G2):
            to = [y_pair]
        else:
            to = []
        for d, peer in enumerate(to):
            send(
                share[s], yb[s].at[pl.ds(d, 1)], y_s.at[s], y_r.at[s], peer,
                (("y", s), yb[s].at[0:len(to)]),
            )

    def scatter(s, stage):
        if stage == 1:
            arrived(cb[s], core_r.at[s], core_s.at[s])
            cb[s][...] += part[s][c]
            if WIDE[s] == 1:
                send(
                    cb[s].at[1 - y_odd], pb[s], pair_s.at[s], pair_r.at[s], y_pair,
                    (("pair", s), pb[s]),
                )
                return
        if WIDE[s] == 1:
            stage -= 1
            if stage == 1:
                arrived(pb[s], pair_r.at[s], pair_s.at[s])
                cb[s][y_odd] += pb[s][...]
        (None, chain_first, chain_second, finish)[stage](s)

    def by_parity(own, far):
        first = jnp.where(y_odd == 0, own, far)
        second = jnp.where(y_odd == 0, far, own)
        return jnp.concatenate([first, second], axis=0)

    def total(s):
        if s in (G0, W1, G1):
            arrived(yb[s].at[0:3], y_r.at[s], y_s.at[s])
            return by_parity(share[s][0] + yb[s][1], yb[s][0] + yb[s][2])
        if s in (W2, G2):
            arrived(yb[s].at[0:1], y_r.at[s], y_s.at[s])
            return by_parity(share[s][0], yb[s][0])
        return share[s][...].reshape(2 * PIECE[s], RANK)

    def spot(i, steps):
        full, count = (wfull[i], PIECE[GATHERED[i]]) if i < 3 else (ffull.at[i - 3], 16)
        return full.at[c, :, pl.ds(pl.multiple_of(line(steps) * count, count), count)]

    def spots(i, count):
        full, rows = (wfull[i], PIECE[GATHERED[i]]) if i < 3 else (ffull.at[i - 3], 16)
        return full.at[c, :, 0:count * rows]

    def gather_send(i, index, origin, steps):
        ref = spot(i, origin)
        group = (0, 0, 1, 1, 2, 2, 2)[index]
        send(ref, ref, gz_s.at[i], gz_r.at[i, group], z_peer[steps], (("gz", i), spots(i, 7)))

    def gather_wait(i, group):
        arrived(spots(i, (2, 2, 3)[group]), gz_r.at[i, group], gz_s.at[i])

    def gather_core(i, origin):
        ref = spot(i, origin)
        send(ref, ref, gc_s.at[i], gc_r.at[i], partner, (("gc", i), spots(i, 8)))

    def gather_put(i, value):
        spot(i, 0)[...] = value.reshape(2, value.shape[0] // 2, RANK)

    def gather_start(i):
        for index, steps in enumerate((2, -2, 1, -1)):
            gather_send(i, index, 0, steps)
        gather_core(i, 0)

    def gather_step(i):
        gather_wait(i, 0)
        gather_send(i, 4, -2, 2)
        gather_send(i, 5, -2, 1)
        gather_send(i, 6, 2, -1)
        gather_core(i, -2)
        gather_core(i, 2)
        gather_wait(i, 1)
        gather_core(i, -1)
        gather_core(i, 1)

    def gather_last(i):
        gather_wait(i, 2)
        for origin in (-4, -3, 3):
            gather_core(i, origin)

    def gather_end(i):
        arrived(spots(i, 8), gc_r.at[i], gc_s.at[i])

    def w_block(l, m):
        full = wfull[l - 1][...].reshape(l * RANK, RANK)
        return split(full[m * RANK:(m + 1) * RANK])

    factors = {}

    def pair(own, sibling, upper):
        return jnp.where(
            upper == 0,
            jnp.concatenate([own, sibling], axis=1),
            jnp.concatenate([sibling, own], axis=1),
        )

    def factor(level, paired):
        value = product(split(paired), split(k_matrix(level)), NT)
        factors[level] = split(value)
        gather_put(3 + level, value)
        if level > 0:
            gather_start(3 + level)

    def to_x():
        xs[...] = total(G0)
        for d in range(3):
            send(xs, xb.at[d], x_s.at[0], x_r.at[0], x_peer[d], ("x", xb))

    def level_0():
        arrived(xb, x_r.at[0], x_s.at[0])
        even = x_odd == 0
        own = xs[...] + jnp.where(even, xb[2], xb[0])
        sibling = xb[1] + jnp.where(even, xb[0], xb[2])
        factor(0, pair(own, sibling, x // 2))

    def level_sums(level):
        value = total((G1, G2, G3)[level - 1])
        for m in range(level):
            value = value - product(factors[m], w_block(level, m), NN)
        sibs[level - 1] = value
        to = (x_pair, y_far, y_pair)[level - 1]
        send(
            sibs.at[level - 1], sib.at[level - 1], sib_s.at[level - 1], sib_r.at[level - 1], to,
            (("sib", level), sib.at[level - 1]),
        )

    def level_factor(level):
        arrived(sib.at[level - 1], sib_r.at[level - 1], sib_s.at[level - 1])
        upper = (x_odd, y // 2, y_odd)[level - 1]
        factor(level, pair(sibs[level - 1], sib[level - 1], upper))

    block = 256
    out_copy = []

    def set_f(level):
        gather_end(3 + level)
        if level == 3:
            loads["u3"].wait()
        high, low = split(ffull[level].reshape(SIDES, RANK))
        f_hi[...] = high
        f_lo[...] = low

    def update(level):
        set_f(level)

        @pl.loop(0, ROWS // block)
        def _(i):
            rows = pl.ds(pl.multiple_of(i * block, block), block)
            solved[rows, :] -= product(split(u_in[level, rows, :]), (f_hi[...], f_lo[...]), NT)

    def w_start(i):
        gather_put(i, total(GATHERED[i]))
        gather_start(i)

    bind = functools.partial
    scatters = {}
    for s in range(NS):
        for stage in range(1, 6 - WIDE[s]):
            scatters.setdefault(s + stage, []).append(bind(scatter, s, stage))
    after = {
        2: [bind(k_step, 0)],
        3: [k_lines_first],
        5: [to_x, k_far],
        6: [bind(w_start, 0), k_near, k_lines_more, bind(k_start, 1)],
        7: [bind(gather_step, 0), bind(w_start, 1), level_0, bind(k_step, 1)],
        8: [bind(gather_step, 1), bind(gather_last, 0), bind(w_start, 2), k_middle],
        9: [
            bind(gather_end, 0), bind(level_sums, 1),
            bind(gather_step, 2), bind(gather_last, 1), bind(gather_start, 3), k_last,
            bind(level_factor, 1),
            bind(gather_end, 1), bind(level_sums, 2),
            bind(gather_last, 2), bind(gather_step, 3),
            bind(level_factor, 2),
            bind(gather_end, 2), bind(level_sums, 3),
            bind(gather_step, 4), bind(gather_last, 3),
            bind(level_factor, 3),
            bind(gather_step, 5), bind(gather_last, 4), bind(update, 0),
            bind(gather_step, 6), bind(gather_last, 5), bind(update, 1),
            bind(gather_last, 6), bind(update, 2), bind(update, 3),
        ],
    }
    for t in range(10):
        for step in scatters.get(t, []):
            step()
        for step in after.get(t, []):
            step()
        if t < NS:
            compute(t)
            if t == 0:
                pl.semaphore_wait(barrier, len(peers))
            core_send(t)
            if t == 0:
                k_start(0)
    for send_sem, recv_sem, ref in drains.values():
        describe(ref, ref, send_sem, recv_sem, partner).wait_send()


def solve(rhs, u, v, *couples):
    dma = pltpu.SemaphoreType.DMA
    any_space = pl.BlockSpec(memory_space=pl.ANY)
    pairs = []
    for sent, received in (
        ((NS,), (NS,)), ((NS,), (NS,)), ((NS,), (NS, 2)), ((NS,), (NS,)), ((1,), (1,)), ((3,), (3,)),
        ((7,), (7, 3)), ((7,), (7,)), ((2,), (2, 3)), ((4,), (4,)), ((4,), (4,)),
    ):
        pairs += [dma(sent), dma(received)]
    vm = pltpu.VMEM
    scratch = [
        vm((4, ROWS, RANK), F32), vm((4, ROWS, RANK), F32),
        vm((1280, ROWS), BF16), vm((1280, ROWS), BF16),
        vm((4, ROWS, RANK), BF16), vm((4, ROWS, RANK), BF16),
    ]
    scratch += [vm((2, 2, q, RANK), F32) for q in QUARTER]
    scratch += [vm((2, q, RANK), F32) for q in QUARTER]
    scratch += [vm((q, RANK), F32) for q in QUARTER]
    scratch += [vm((7, w, h, RANK), F32) for w, h in zip(WIDE, PIECE)]
    scratch += [vm((w, h, RANK), F32) for w, h in zip(WIDE, PIECE)]
    scratch += [vm((3, h, RANK), F32) for h in PIECE]
    scratch += [vm((3, 32, RANK), F32), vm((32, RANK), F32)]
    scratch += [vm((2, 2, QUARTER[s], RANK), F32) for s in GATHERED]
    scratch += [
        vm((4, 2, 2, 128, RANK), F32), vm((SIDES, RANK), BF16), vm((SIDES, RANK), BF16),
        vm((3, 32, RANK), F32), vm((3, 32, RANK), F32),
        vm((2, 64, 128), F32), vm((8, 56, 128), F32),
        vm((8, 8, 2, 8, 128), F32), vm((4, 8, 2, 16, 128), F32),
        vm((2, 8, 2, 32, 128), F32), vm((1, 8, 2, 64, 128), F32),
        vm((4 * RANK, 128), F32),
        dma((9,)),
    ]
    return pl.pallas_call(
        solve_kernel,
        out_shape=pltpu.VMEM((ROWS, SIDES), F32),
        in_specs=[any_space] * 3 + [pl.BlockSpec(memory_space=pltpu.VMEM)] * 4,
        out_specs=pl.BlockSpec(memory_space=pltpu.VMEM),
        scratch_shapes=scratch + pairs,
        compiler_params=pltpu.CompilerParams(
            collective_id=0, has_side_effects=True, vmem_limit_bytes=61 * 1024 * 1024
        ),
        name="solve",
    )(rhs, u, v, *couples)


def solution(mesh):
    placed = (
        P(("rows", "sub"), None),
        P(None, ("rows", "sub"), None),
        P(None, ("rows", "sub"), None),
        P(("rows", "sub"), None),
        P(("rows", "sub"), None),
        P(("rows", "sub"), None),
        P(("rows", "sub"), None),
    )
    return jax.shard_map(
        solve, mesh=mesh, in_specs=placed, out_specs=P(("rows", "sub"), None), check_vma=False
    )
```

```python
import functools

import jax
import jax.numpy as jnp
from jax import lax
from jax.experimental import pallas as pl
from jax.experimental.pallas import tpu as pltpu
from jax.sharding import PartitionSpec as P

F32 = jnp.float32
BF16 = jnp.bfloat16
MESH = pl.DeviceIdType.MESH

RANK = 256
SIDES = 512
ROWS = 1024
STREAMS = (
    (512, 256, 1, True),
    (512, 512, 2, True),
    (0, 512, 0, True),
    (512, 768, 3, False),
    (0, 512, 1, True),
    (0, 512, 2, True),
    (0, 512, 3, False),
)
W1, W2, G0, W3, G1, G2, G3 = range(7)
NS = len(STREAMS)
QUARTER = tuple(rows // 4 for _, rows, _, _ in STREAMS)
PIECE = tuple(rows // 32 for _, rows, _, _ in STREAMS)
WIDE = tuple(1 if paired else 2 for _, _, _, paired in STREAMS)
GATHERED = (W1, W2, W3)
KROWS = (8, 16, 32, 64)
KOFF = (0, 8, 24)


def split(value):
    high = value.astype(BF16)
    return high, (value - high.astype(F32)).astype(BF16)


def product(left, right, dims):
    def one(a, b):
        return lax.dot_general(a, b, (dims, ((), ())), preferred_element_type=F32)

    return one(left[0], right[0]) + (one(left[0], right[1]) + one(left[1], right[0]))


NN = ((1,), (0,))
NT = ((1,), (1,))


def solve_kernel(*refs):
    refs = list(refs)

    def take(count=None):
        if count is None:
            return refs.pop(0)
        return [refs.pop(0) for _ in range(count)]

    rhs_hbm, u_hbm, v_hbm = take(3)
    k_own = take(4)
    solved = take()
    u_in, v_in, a_hi, a_lo, v_hi, v_lo, u_hi, u_lo = take(8)
    part, cb, pb, rz, share, yb = [take(NS) for _ in range(6)]
    xb, xs = take(2)
    wfull = take(3)
    ffull, f_hi, f_lo, sibs, sib = take(5)
    kown, kz, k0, k1, k2, k3, kflat = take(7)
    in_sem = take()
    (core_s, core_r, pair_s, pair_r, z_s, z_r, y_s, y_r, x_s, x_r, sib_s, sib_r,
     gz_s, gz_r, gc_s, gc_r, kz_s, kz_r, kf_s, kf_r, kc_s, kc_r) = take(22)
    assert not refs

    row_index = lax.axis_index("rows")
    sub_index = lax.axis_index("sub")
    x = row_index // 16
    y = row_index // 4 % 4
    z = row_index % 4 * 2 + sub_index // 2
    c = sub_index % 2
    way = 1 - 2 * c

    def line(steps):
        return (z + way * steps + 16) % 8

    def device(x, y, z, c):
        return (x * 16 + y * 4 + z // 2, z % 2 * 2 + c)

    partner = device(x, y, z, 1 - c)
    z_peer = {steps: device(x, y, line(steps), c) for steps in (1, -1, 2, -2)}
    y_peer = [device(x, (y + d) % 4, z, c) for d in (1, 2, 3)]
    x_peer = [device((x + d) % 4, y, z, c) for d in (1, 2, 3)]
    y_odd, x_odd = y % 2, x % 2
    y_pair = device(x, y + 1 - 2 * y_odd, z, c)
    x_pair = device(x + 1 - 2 * x_odd, y, z, c)
    y_far = device(x, 3 - y, z, c)

    def describe(src, dst, s, r, to):
        return pltpu.make_async_remote_copy(
            src_ref=src, dst_ref=dst, send_sem=s, recv_sem=r, device_id=to, device_id_type=MESH
        )

    drains = {}

    def send(src, dst, s, r, to, drain):
        describe(src, dst, s, r, to).start()
        key, ref = drain
        drains[key] = (s, r, ref)

    def arrived(ref, r, s):
        describe(ref, ref, s, r, partner).wait_recv()

    barrier = pltpu.get_barrier_semaphore()
    peers = [partner] + list(z_peer.values()) + y_peer + x_peer
    for peer in peers:
        pl.semaphore_signal(barrier, inc=1, device_id=peer, device_id_type=MESH)

    loads = {}

    def load(name, src, dst, index):
        copy = pltpu.make_async_copy(src, dst, in_sem.at[index])
        copy.start()
        loads[name] = copy

    def load_group(*names):
        for name in names:
            index = ("u0", "v1", "u1", "v2", "rhs", "v0", "u2", "v3", "u3").index(name)
            if name == "rhs":
                load(name, rhs_hbm, solved, index)
            else:
                src, dst = (u_hbm, u_in) if name[0] == "u" else (v_hbm, v_in)
                load(name, src.at[int(name[1])], dst.at[int(name[1])], index)

    load_group("u0", "v1")

    kasm = (k0, k1, k2, k3)
    kline = (x_odd * 4 + y, y, y_odd, 0)

    def k_piece(which, origin):
        return kz.at[origin] if which == 0 else k3.at[0, origin, c]

    def k_send(which, index, origin, steps):
        ref = k_piece(which, origin)
        group = (0, 0, 1, 1, 2, 2, 2)[index]
        every = kz.at[0:7] if which == 0 else k3.at[0, 0:7, c]
        send(ref, ref, kz_s.at[which], kz_r.at[which, group], z_peer[steps], (("kz", which), every))

    def k_wait(which, group):
        count = (2, 2, 3)[group]
        ref = kz.at[0:count] if which == 0 else k3.at[0, 0:count, c]
        arrived(ref, kz_r.at[which, group], kz_s.at[which])

    def k_start(which):
        for level in (0, 1, 2) if which == 0 else (3,):
            count = KROWS[level] // 4
            for b in range(4):
                place = pl.ds(KOFF[level] + b if level < 3 else b, count, stride=4)
                kown[which, place, :] = k_own[level][:, b * 128:(b + 1) * 128]
        if which == 0:
            kz[z] = kown[0, 0:56, :]
        else:
            k3[0, z, c] = kown[1]
        for index, steps in enumerate((2, -2, 1, -1)):
            k_send(which, index, z, steps)

    def k_step(which):
        k_wait(which, 0)
        k_send(which, 4, line(-2), 2)
        k_send(which, 5, line(-2), 1)
        k_send(which, 6, line(2), -1)

    def k_end(which):
        k_wait(which, 1)
        k_wait(which, 2)

    def k_core(level):
        ref = kasm[level].at[:, :, c]
        send(ref, ref, kc_s.at[level], kc_r.at[level], partner, (("kc", level), ref))

    def k_lines_first():
        k_end(0)
        for level in range(3):
            kasm[level][kline[level], :, c] = kz[:, KOFF[level]:KOFF[level] + KROWS[level]]
        for d in range(3):
            send(
                kz.at[:, 0:8], k0.at[kline[0], :, c], kf_s.at[0], kf_r.at[0], y_peer[d],
                ("kf0", k0.at[0:3, :, c]),
            )

    def k_lines_more():
        for d in range(3):
            send(
                kz.at[:, 8:24], k1.at[kline[1], :, c], kf_s.at[1], kf_r.at[1], y_peer[d],
                ("kf1", k1.at[0:3, :, c]),
            )

    def k_lines_last():
        send(
            kz.at[:, 24:56], k2.at[kline[2], :, c], kf_s.at[2], kf_r.at[2], y_pair,
            ("kf2", k2.at[0, :, c]),
        )

    def k_far():
        arrived(k0.at[0:3, :, c], kf_r.at[0], kf_s.at[0])
        ref = k0.at[pl.ds(x_odd * 4, 4), :, c]
        send(ref, ref, kf_s.at[3], kf_r.at[3], x_pair, ("kf3", ref))

    def k_near():
        arrived(k0.at[0:4, :, c], kf_r.at[3], kf_s.at[3])
        k_core(0)

    def k_middle():
        arrived(k1.at[0:3, :, c], kf_r.at[1], kf_s.at[1])
        k_core(1)

    def k_pair():
        arrived(k2.at[0, :, c], kf_r.at[2], kf_s.at[2])
        k_core(2)

    def k_last():
        k_end(1)
        k_core(3)

    def k_matrix(level):
        arrived(kasm[level].at[:, :, c], kc_r.at[level], kc_s.at[level])
        kflat[...] = kasm[level][...].reshape(4 * RANK, 128)
        return jnp.concatenate([kflat[pl.ds(b, RANK, stride=4), :] for b in range(4)], axis=1)

    def set_a(value, first):
        turned = jnp.transpose(value)
        high, low = split(turned)
        a_hi[first:first + value.shape[1], :] = high
        a_lo[first:first + value.shape[1], :] = low

    def set_v(level):
        loads["v%d" % level].wait()
        high, low = split(v_in[level])
        v_hi[level] = high
        v_lo[level] = low

    def set_u(level):
        loads["u%d" % level].wait()
        if level < 3:
            set_a(u_in[level], 512 + RANK * level)
        high, low = split(u_in[level])
        u_hi[level] = high
        u_lo[level] = low

    def compute(s):
        if s == W1:
            set_u(0)
            load_group("u1", "v2", "rhs")
            set_v(1)
        elif s == W2:
            set_u(1)
            load_group("v0", "u2", "v3")
            set_v(2)
        elif s == G0:
            loads["rhs"].wait()
            load_group("u3")
            set_a(solved[...], 0)
            set_v(0)
        elif s == W3:
            set_u(2)
            set_v(3)
        first, rows, level, _ = STREAMS[s]
        for index in range(rows // RANK):
            own = slice(first + index * RANK, first + (index + 1) * RANK)
            value = product((a_hi[own, :], a_lo[own, :]), (v_hi[level], v_lo[level]), NN)
            count = min(QUARTER[s], RANK // 4 if rows != 512 else RANK // 2)
            for at in range(0, RANK, count):
                c_at, rest = divmod(index * RANK + at, 2 * QUARTER[s])
                p_at, row = divmod(rest, QUARTER[s])
                part[s][c_at, p_at, row:row + count, :] = value[at:at + count]

    def core_send(s):
        send(part[s].at[1 - c], cb[s], core_s.at[s], core_r.at[s], partner, (("core", s), cb[s]))

    def piece(s, steps):
        lines = pl.ds(y_odd, 1) if WIDE[s] == 1 else pl.ds(0, 2)
        count = PIECE[s]
        return cb[s].at[lines, pl.ds(pl.multiple_of(line(steps) * count, count), count)]

    def z_send(s, src, index, steps):
        group = 0 if index < 3 else 1
        send(src, rz[s].at[index], z_s.at[s], z_r.at[s, group], z_peer[steps], (("z", s), rz[s]))

    def chain_first(s):
        z_send(s, piece(s, 4), 1, 2)
        z_send(s, piece(s, 3), 0, 1)
        z_send(s, piece(s, -3), 2, -1)
        z_send(s, piece(s, 1), 3, 1)
        z_send(s, piece(s, -1), 4, -1)

    def chain_second(s):
        arrived(rz[s].at[0:3], z_r.at[s, 0], z_s.at[s])
        rz[s][0] = (rz[s][0] + rz[s][1]) + piece(s, 2)[...]
        z_send(s, rz[s].at[0], 5, 2)
        rz[s][2] += piece(s, -2)[...]
        z_send(s, rz[s].at[2], 6, -2)

    def finish(s):
        arrived(rz[s].at[3:7], z_r.at[s, 1], z_s.at[s])
        share[s][...] = piece(s, 0)[...] + ((rz[s][3] + rz[s][4]) + (rz[s][5] + rz[s][6]))
        if s in (G0, W1, G1):
            to = y_peer
        elif s in (W2, G2):
            to = [y_pair]
        else:
            to = []
        for d, peer in enumerate(to):
            send(
                share[s], yb[s].at[pl.ds(d, 1)], y_s.at[s], y_r.at[s], peer,
                (("y", s), yb[s].at[0:len(to)]),
            )

    def scatter(s, stage):
        if stage == 1:
            arrived(cb[s], core_r.at[s], core_s.at[s])
            cb[s][...] += part[s][c]
            if WIDE[s] == 1:
                send(
                    cb[s].at[1 - y_odd], pb[s], pair_s.at[s], pair_r.at[s], y_pair,
                    (("pair", s), pb[s]),
                )
                return
        if WIDE[s] == 1:
            stage -= 1
            if stage == 1:
                arrived(pb[s], pair_r.at[s], pair_s.at[s])
                cb[s][y_odd] += pb[s][...]
        (None, chain_first, chain_second, finish)[stage](s)

    def by_parity(own, far):
        first = jnp.where(y_odd == 0, own, far)
        second = jnp.where(y_odd == 0, far, own)
        return jnp.concatenate([first, second], axis=0)

    def total(s):
        if s in (G0, W1, G1):
            arrived(yb[s].at[0:3], y_r.at[s], y_s.at[s])
            return by_parity(share[s][0] + yb[s][1], yb[s][0] + yb[s][2])
        if s in (W2, G2):
            arrived(yb[s].at[0:1], y_r.at[s], y_s.at[s])
            return by_parity(share[s][0], yb[s][0])
        return share[s][...].reshape(2 * PIECE[s], RANK)

    def spot(i, steps):
        full, count = (wfull[i], PIECE[GATHERED[i]]) if i < 3 else (ffull.at[i - 3], 16)
        return full.at[c, :, pl.ds(pl.multiple_of(line(steps) * count, count), count)]

    def spots(i, count):
        full, rows = (wfull[i], PIECE[GATHERED[i]]) if i < 3 else (ffull.at[i - 3], 16)
        return full.at[c, :, 0:count * rows]

    def gather_send(i, index, origin, steps):
        ref = spot(i, origin)
        group = (0, 0, 1, 1, 2, 2, 2)[index]
        send(ref, ref, gz_s.at[i], gz_r.at[i, group], z_peer[steps], (("gz", i), spots(i, 7)))

    def gather_wait(i, group):
        arrived(spots(i, (2, 2, 3)[group]), gz_r.at[i, group], gz_s.at[i])

    def gather_core(i, origin):
        ref = spot(i, origin)
        send(ref, ref, gc_s.at[i], gc_r.at[i], partner, (("gc", i), spots(i, 8)))

    def gather_put(i, value):
        spot(i, 0)[...] = value.reshape(2, value.shape[0] // 2, RANK)

    def gather_start(i):
        for index, steps in enumerate((2, -2, 1, -1)):
            gather_send(i, index, 0, steps)
        gather_core(i, 0)

    def gather_step(i):
        gather_wait(i, 0)
        gather_send(i, 4, -2, 2)
        gather_send(i, 5, -2, 1)
        gather_send(i, 6, 2, -1)
        gather_core(i, -2)
        gather_core(i, 2)
        gather_wait(i, 1)
        gather_core(i, -1)
        gather_core(i, 1)

    def gather_last(i):
        gather_wait(i, 2)
        for origin in (-4, -3, 3):
            gather_core(i, origin)

    def gather_end(i):
        arrived(spots(i, 8), gc_r.at[i], gc_s.at[i])

    def w_block(full, l, m):
        return split(full[l - 1][...].reshape(l * RANK, RANK)[m * RANK:(m + 1) * RANK])

    sibling = (x_pair, y_far, y_pair)

    factors = {}

    def pair(own, sibling, upper):
        return jnp.where(
            upper == 0,
            jnp.concatenate([own, sibling], axis=1),
            jnp.concatenate([sibling, own], axis=1),
        )

    def factor(level, paired):
        value = product(split(paired), split(k_matrix(level)), NT)
        factors[level] = split(value)
        gather_put(3 + level, value)
        if level > 0:
            gather_start(3 + level)

    def to_x():
        xs[...] = total(G0)
        for d in range(3):
            send(xs, xb.at[d], x_s.at[0], x_r.at[0], x_peer[d], ("x", xb))

    def level_0():
        arrived(xb, x_r.at[0], x_s.at[0])
        even = x_odd == 0
        own = xs[...] + jnp.where(even, xb[2], xb[0])
        sibling = xb[1] + jnp.where(even, xb[0], xb[2])
        factor(0, pair(own, sibling, x // 2))

    def own_sums(level):
        gather_end(level - 1)
        own = sibs[level - 1]
        for m in range(level):
            own = own - product(factors[m], w_block(wfull, level, m), NN)
        return own

    def sums_of(level):
        sibs[level - 1] = total((G1, G2, G3)[level - 1])

    def exchange(level):
        i = level - 1
        send(sibs.at[i], sib.at[i], sib_s.at[i], sib_r.at[i], sibling[i], (("sib", level), sib.at[i]))

    def level_sums(level):
        sibs[level - 1] = own_sums(level)
        exchange(level)

    def level_factor(level):
        i = level - 1
        arrived(sib.at[i], sib_r.at[i], sib_s.at[i])
        factor(level, pair(sibs[i], sib[i], (x_odd, y // 2, y_odd)[i]))

    block = 256

    def update(level):
        gather_end(3 + level)
        high, low = split(ffull[level].reshape(SIDES, RANK))
        f_hi[...] = high
        f_lo[...] = low
        for i in range(ROWS // block):
            rows = pl.ds(i * block, block)
            solved[rows, :] -= product(
                (u_hi[level, rows, :], u_lo[level, rows, :]), (f_hi[...], f_lo[...]), NT
            )

    def update_half(near):
        core = c if near else 1 - c
        if not near:
            gather_end(6)
        high, low = split(ffull[3, core].reshape(RANK, RANK))
        place = slice(0, RANK) if near else slice(RANK, SIDES)
        f_hi[place, :] = high
        f_lo[place, :] = low
        columns = pl.ds(pl.multiple_of(core * RANK, RANK), RANK)
        for i in range(ROWS // block):
            rows = pl.ds(i * block, block)
            solved[rows, columns] -= product(
                (u_hi[3, rows, :], u_lo[3, rows, :]), (f_hi[place, :], f_lo[place, :]), NT
            )

    def w_start(i):
        gather_put(i, total(GATHERED[i]))
        gather_start(i)

    bind = functools.partial
    def make(s):
        compute(s)
        core_send(s)

    def sc(s, stage):
        return bind(scatter, s, stage)

    def enter():
        pl.semaphore_wait(barrier, len(peers))
        core_send(W1)
        core_send(W2)
        k_start(0)

    order = [
        bind(compute, W1), bind(compute, W2), enter, bind(k_start, 1),
        sc(W1, 1), bind(make, G0), sc(W2, 1),
        bind(make, W3), sc(W1, 2), bind(k_step, 0), sc(G0, 1), sc(W3, 1),
        bind(make, G1), sc(W2, 2), bind(make, G2), bind(k_step, 1), sc(G1, 1), sc(W1, 3),
        bind(make, G3), k_lines_first, sc(G0, 2), sc(G2, 1), sc(W2, 3), sc(W1, 4),
        sc(W3, 2), sc(G3, 1), sc(G1, 2), sc(G0, 3), k_far, k_last, sc(W2, 4), bind(w_start, 0),
        sc(G2, 2), sc(G0, 4), sc(G1, 3), k_lines_more, bind(set_u, 3),
        bind(w_start, 1), bind(gather_step, 0), sc(W3, 3), to_x, sc(G2, 3), sc(G1, 4),
        bind(w_start, 2), k_near,
        bind(gather_last, 0), bind(gather_step, 1), sc(G2, 4), bind(sums_of, 1), k_lines_last,
        level_0, bind(gather_step, 2), sc(G3, 2), bind(level_sums, 1),
        bind(gather_last, 1), k_middle, bind(sums_of, 2), bind(gather_last, 2),
        bind(level_factor, 1), k_pair, bind(level_sums, 2), sc(G3, 3), bind(gather_start, 3),
        bind(level_factor, 2), bind(sums_of, 3), bind(level_sums, 3),
        bind(gather_step, 4), bind(gather_step, 3), bind(level_factor, 3),
        bind(gather_step, 5), bind(gather_last, 4), bind(gather_last, 3),
        bind(gather_step, 6), bind(update, 1), bind(update, 0),
        bind(gather_last, 5), bind(gather_last, 6), bind(update, 2),
        bind(update_half, True), bind(update_half, False),
    ]
    for step in order:
        step()
    for send_sem, recv_sem, ref in drains.values():
        describe(ref, ref, send_sem, recv_sem, partner).wait_send()


def solve(rhs, u, v, *couples):
    dma = pltpu.SemaphoreType.DMA
    any_space = pl.BlockSpec(memory_space=pl.ANY)
    pairs = []
    for sent, received in (
        ((NS,), (NS,)), ((NS,), (NS,)), ((NS,), (NS, 2)), ((NS,), (NS,)), ((1,), (1,)), ((3,), (3,)),
        ((7,), (7, 3)), ((7,), (7,)), ((2,), (2, 3)), ((4,), (4,)), ((4,), (4,)),
    ):
        pairs += [dma(sent), dma(received)]
    vm = pltpu.VMEM
    scratch = [
        vm((4, ROWS, RANK), F32), vm((4, ROWS, RANK), F32),
        vm((1280, ROWS), BF16), vm((1280, ROWS), BF16),
        vm((4, ROWS, RANK), BF16), vm((4, ROWS, RANK), BF16),
        vm((4, ROWS, RANK), BF16), vm((4, ROWS, RANK), BF16),
    ]
    scratch += [vm((2, 2, q, RANK), F32) for q in QUARTER]
    scratch += [vm((2, q, RANK), F32) for q in QUARTER]
    scratch += [vm((q, RANK), F32) for q in QUARTER]
    scratch += [vm((7, w, h, RANK), F32) for w, h in zip(WIDE, PIECE)]
    scratch += [vm((w, h, RANK), F32) for w, h in zip(WIDE, PIECE)]
    scratch += [vm((3, h, RANK), F32) for h in PIECE]
    scratch += [vm((3, 32, RANK), F32), vm((32, RANK), F32)]
    scratch += [vm((2, 2, QUARTER[s], RANK), F32) for s in GATHERED]
    scratch += [
        vm((4, 2, 2, 128, RANK), F32), vm((SIDES, RANK), BF16), vm((SIDES, RANK), BF16),
        vm((3, 32, RANK), F32), vm((3, 32, RANK), F32),
        vm((2, 64, 128), F32), vm((8, 56, 128), F32),
        vm((8, 8, 2, 8, 128), F32), vm((4, 8, 2, 16, 128), F32),
        vm((2, 8, 2, 32, 128), F32), vm((1, 8, 2, 64, 128), F32),
        vm((4 * RANK, 128), F32),
        dma((9,)),
    ]
    return pl.pallas_call(
        solve_kernel,
        out_shape=pltpu.VMEM((ROWS, SIDES), F32),
        in_specs=[any_space] * 3 + [pl.BlockSpec(memory_space=pltpu.VMEM)] * 4,
        out_specs=pl.BlockSpec(memory_space=pltpu.VMEM),
        scratch_shapes=scratch + pairs,
        compiler_params=pltpu.CompilerParams(
            collective_id=0, has_side_effects=True, vmem_limit_bytes=61 * 1024 * 1024
        ),
        name="solve",
    )(rhs, u, v, *couples)


def solution(mesh):
    placed = (
        P(("rows", "sub"), None),
        P(None, ("rows", "sub"), None),
        P(None, ("rows", "sub"), None),
        P(("rows", "sub"), None),
        P(("rows", "sub"), None),
        P(("rows", "sub"), None),
        P(("rows", "sub"), None),
    )
    return jax.shard_map(
        solve, mesh=mesh, in_specs=placed, out_specs=P(("rows", "sub"), None), check_vma=False
    )
```

```python
import functools

import jax
import jax.numpy as jnp
from jax import lax
from jax.experimental import pallas as pl
from jax.experimental.pallas import tpu as pltpu
from jax.sharding import PartitionSpec as P

F32 = jnp.float32
BF16 = jnp.bfloat16
MESH = pl.DeviceIdType.MESH

RANK = 256
SIDES = 512
ROWS = 1024
STREAMS = (
    (512, 256, 1, True),
    (512, 512, 2, True),
    (0, 512, 0, True),
    (512, 768, 3, False),
    (0, 512, 1, True),
    (0, 512, 2, True),
    (0, 512, 3, False),
)
W1, W2, G0, W3, G1, G2, G3 = range(7)
NS = len(STREAMS)
QUARTER = tuple(rows // 4 for _, rows, _, _ in STREAMS)
PIECE = tuple(rows // 32 for _, rows, _, _ in STREAMS)
WIDE = tuple(1 if paired else 2 for _, _, _, paired in STREAMS)
GATHERED = (W1, W2, W3)
KROWS = (8, 16, 32, 64)
KOFF = (0, 8, 24)


def split(value):
    high = value.astype(BF16)
    return high, (value - high.astype(F32)).astype(BF16)


def product(left, right, dims):
    def one(a, b):
        return lax.dot_general(a, b, (dims, ((), ())), preferred_element_type=F32)

    return one(left[0], right[0]) + (one(left[0], right[1]) + one(left[1], right[0]))


NN = ((1,), (0,))
NT = ((1,), (1,))


def solve_kernel(*refs):
    refs = list(refs)

    def take(count=None):
        if count is None:
            return refs.pop(0)
        return [refs.pop(0) for _ in range(count)]

    rhs_hbm, u_hbm, v_hbm = take(3)
    k_own = take(4)
    solved = take()
    u_in, v_in, a_hi, a_lo, v_hi, v_lo, u_hi, u_lo = take(8)
    part, cb, pb, rz, share, yb = [take(NS) for _ in range(6)]
    xb, xs = take(2)
    wfull = take(3)
    ffull, f_hi, f_lo, sibs, sib = take(5)
    kown, kz, k0, k1, k2, k3, kflat = take(7)
    in_sem = take()
    (core_s, core_r, pair_s, pair_r, z_s, z_r, y_s, y_r, x_s, x_r, sib_s, sib_r,
     gz_s, gz_r, gc_s, gc_r, kz_s, kz_r, kf_s, kf_r, kc_s, kc_r) = take(22)
    assert not refs

    row_index = lax.axis_index("rows")
    sub_index = lax.axis_index("sub")
    x = row_index // 16
    y = row_index // 4 % 4
    z = row_index % 4 * 2 + sub_index // 2
    c = sub_index % 2
    way = 1 - 2 * c

    def line(steps):
        return (z + way * steps + 16) % 8

    def device(x, y, z, c):
        return (x * 16 + y * 4 + z // 2, z % 2 * 2 + c)

    partner = device(x, y, z, 1 - c)
    z_peer = {steps: device(x, y, line(steps), c) for steps in (1, -1, 2, -2)}
    y_peer = [device(x, (y + d) % 4, z, c) for d in (1, 2, 3)]
    x_peer = [device((x + d) % 4, y, z, c) for d in (1, 2, 3)]
    y_odd, x_odd = y % 2, x % 2
    y_pair = device(x, y + 1 - 2 * y_odd, z, c)
    x_pair = device(x + 1 - 2 * x_odd, y, z, c)
    y_far = device(x, 3 - y, z, c)

    def describe(src, dst, s, r, to):
        return pltpu.make_async_remote_copy(
            src_ref=src, dst_ref=dst, send_sem=s, recv_sem=r, device_id=to, device_id_type=MESH
        )

    drains = {}

    def send(src, dst, s, r, to, drain):
        describe(src, dst, s, r, to).start()
        key, ref = drain
        drains[key] = (s, r, ref)

    def arrived(ref, r, s):
        describe(ref, ref, s, r, partner).wait_recv()

    barrier = pltpu.get_barrier_semaphore()
    peers = [partner] + list(z_peer.values()) + y_peer + x_peer
    for peer in peers:
        pl.semaphore_signal(barrier, inc=1, device_id=peer, device_id_type=MESH)

    loads = {}

    def load(name, src, dst, index):
        copy = pltpu.make_async_copy(src, dst, in_sem.at[index])
        copy.start()
        loads[name] = copy

    def load_group(*names):
        for name in names:
            index = ("u0", "v1", "u1", "v2", "rhs", "v0", "u2", "v3", "u3").index(name)
            if name == "rhs":
                load(name, rhs_hbm, solved, index)
            else:
                src, dst = (u_hbm, u_in) if name[0] == "u" else (v_hbm, v_in)
                load(name, src.at[int(name[1])], dst.at[int(name[1])], index)

    load_group("u0", "v1")

    kasm = (k0, k1, k2, k3)
    kline = (x_odd * 4 + y, y, y_odd, 0)

    def k_piece(which, origin):
        return kz.at[origin] if which == 0 else k3.at[0, origin, c]

    def k_send(which, index, origin, steps):
        ref = k_piece(which, origin)
        group = (0, 0, 1, 1, 2, 2, 2)[index]
        every = kz.at[0:7] if which == 0 else k3.at[0, 0:7, c]
        send(ref, ref, kz_s.at[which], kz_r.at[which, group], z_peer[steps], (("kz", which), every))

    def k_wait(which, group):
        count = (2, 2, 3)[group]
        ref = kz.at[0:count] if which == 0 else k3.at[0, 0:count, c]
        arrived(ref, kz_r.at[which, group], kz_s.at[which])

    def k_start(which):
        for level in (0, 1, 2) if which == 0 else (3,):
            count = KROWS[level] // 4
            for b in range(4):
                place = pl.ds(KOFF[level] + b if level < 3 else b, count, stride=4)
                kown[which, place, :] = k_own[level][:, b * 128:(b + 1) * 128]
        if which == 0:
            kz[z] = kown[0, 0:56, :]
        else:
            k3[0, z, c] = kown[1]
        for index, steps in enumerate((2, -2, 1, -1)):
            k_send(which, index, z, steps)

    def k_step(which):
        k_wait(which, 0)
        k_send(which, 4, line(-2), 2)
        k_send(which, 5, line(-2), 1)
        k_send(which, 6, line(2), -1)

    def k_end(which):
        k_wait(which, 1)
        k_wait(which, 2)

    def k_core(level):
        ref = kasm[level].at[:, :, c]
        send(ref, ref, kc_s.at[level], kc_r.at[level], partner, (("kc", level), ref))

    def k_lines_first():
        k_end(0)
        for level in range(3):
            kasm[level][kline[level], :, c] = kz[:, KOFF[level]:KOFF[level] + KROWS[level]]
        for d in range(3):
            send(
                kz.at[:, 0:8], k0.at[kline[0], :, c], kf_s.at[0], kf_r.at[0], y_peer[d],
                ("kf0", k0.at[0:3, :, c]),
            )

    def k_lines_more():
        for d in range(3):
            send(
                kz.at[:, 8:24], k1.at[kline[1], :, c], kf_s.at[1], kf_r.at[1], y_peer[d],
                ("kf1", k1.at[0:3, :, c]),
            )

    def k_lines_last():
        send(
            kz.at[:, 24:56], k2.at[kline[2], :, c], kf_s.at[2], kf_r.at[2], y_pair,
            ("kf2", k2.at[0, :, c]),
        )

    def k_far():
        arrived(k0.at[0:3, :, c], kf_r.at[0], kf_s.at[0])
        ref = k0.at[pl.ds(x_odd * 4, 4), :, c]
        send(ref, ref, kf_s.at[3], kf_r.at[3], x_pair, ("kf3", ref))

    def k_near():
        arrived(k0.at[0:4, :, c], kf_r.at[3], kf_s.at[3])
        k_core(0)

    def k_middle():
        arrived(k1.at[0:3, :, c], kf_r.at[1], kf_s.at[1])
        k_core(1)

    def k_pair():
        arrived(k2.at[0, :, c], kf_r.at[2], kf_s.at[2])
        k_core(2)

    def k_last():
        k_end(1)
        k_core(3)

    def k_matrix(level):
        arrived(kasm[level].at[:, :, c], kc_r.at[level], kc_s.at[level])
        kflat[...] = kasm[level][...].reshape(4 * RANK, 128)
        return jnp.concatenate([kflat[pl.ds(b, RANK, stride=4), :] for b in range(4)], axis=1)

    def set_a(value, first):
        turned = jnp.transpose(value)
        high, low = split(turned)
        a_hi[first:first + value.shape[1], :] = high
        a_lo[first:first + value.shape[1], :] = low

    def set_v(level):
        loads["v%d" % level].wait()
        high, low = split(v_in[level])
        v_hi[level] = high
        v_lo[level] = low

    def set_u(level):
        loads["u%d" % level].wait()
        if level < 3:
            set_a(u_in[level], 512 + RANK * level)
        high, low = split(u_in[level])
        u_hi[level] = high
        u_lo[level] = low

    def compute(s):
        if s == W1:
            set_u(0)
            load_group("u1", "v2", "rhs")
            set_v(1)
        elif s == W2:
            set_u(1)
            load_group("v0", "u2", "v3")
            set_v(2)
        elif s == G0:
            loads["rhs"].wait()
            load_group("u3")
            set_a(solved[...], 0)
            set_v(0)
        elif s == W3:
            set_u(2)
            set_v(3)
        first, rows, level, _ = STREAMS[s]
        for index in range(rows // RANK):
            own = slice(first + index * RANK, first + (index + 1) * RANK)
            value = product((a_hi[own, :], a_lo[own, :]), (v_hi[level], v_lo[level]), NN)
            count = min(QUARTER[s], RANK // 4 if rows != 512 else RANK // 2)
            for at in range(0, RANK, count):
                c_at, rest = divmod(index * RANK + at, 2 * QUARTER[s])
                p_at, row = divmod(rest, QUARTER[s])
                part[s][c_at, p_at, row:row + count, :] = value[at:at + count]

    def core_send(s):
        send(part[s].at[1 - c], cb[s], core_s.at[s], core_r.at[s], partner, (("core", s), cb[s]))

    def piece(s, steps):
        lines = pl.ds(y_odd, 1) if WIDE[s] == 1 else pl.ds(0, 2)
        count = PIECE[s]
        return cb[s].at[lines, pl.ds(pl.multiple_of(line(steps) * count, count), count)]

    def z_send(s, src, index, steps):
        group = 0 if index < 3 else 1
        send(src, rz[s].at[index], z_s.at[s], z_r.at[s, group], z_peer[steps], (("z", s), rz[s]))

    def chain_first(s):
        z_send(s, piece(s, 4), 1, 2)
        z_send(s, piece(s, 3), 0, 1)
        z_send(s, piece(s, -3), 2, -1)
        z_send(s, piece(s, 1), 3, 1)
        z_send(s, piece(s, -1), 4, -1)

    def chain_second(s):
        arrived(rz[s].at[0:3], z_r.at[s, 0], z_s.at[s])
        rz[s][0] = (rz[s][0] + rz[s][1]) + piece(s, 2)[...]
        z_send(s, rz[s].at[0], 5, 2)
        rz[s][2] += piece(s, -2)[...]
        z_send(s, rz[s].at[2], 6, -2)

    def long_chain(s, k):
        if k > 1:
            arrived(rz[s].at[0:2], z_r.at[s, k - 2], z_s.at[s])
            rz[s][k - 2] += piece(s, 5 - k)[...]
        if 1 < k <= 3:
            rz[s][k + 2] += piece(s, k - 4)[...]
        drain = (("z", s), rz[s])
        up = piece(s, 4) if k == 1 else rz[s].at[k - 2]
        send(up, rz[s].at[k - 1], z_s.at[s], z_r.at[s, k - 1], z_peer[1], drain)
        if k <= 3:
            down = piece(s, -3) if k == 1 else rz[s].at[k + 2]
            send(down, rz[s].at[k + 3], z_s.at[s], z_r.at[s, k - 1], z_peer[-1], drain)

    def finish(s):
        if WIDE[s] == 1:
            arrived(rz[s].at[3:7], z_r.at[s, 1], z_s.at[s])
            share[s][...] = piece(s, 0)[...] + ((rz[s][3] + rz[s][4]) + (rz[s][5] + rz[s][6]))
        else:
            arrived(rz[s].at[0:1], z_r.at[s, 3], z_s.at[s])
            share[s][...] = piece(s, 0)[...] + (rz[s][3] + rz[s][6])
        if s in (G0, W1, G1):
            to = y_peer
        elif s in (W2, G2):
            to = [y_pair]
        else:
            to = []
        for d, peer in enumerate(to):
            send(
                share[s], yb[s].at[pl.ds(d, 1)], y_s.at[s], y_r.at[s], peer,
                (("y", s), yb[s].at[0:len(to)]),
            )

    def scatter(s, stage):
        if stage == 1:
            arrived(cb[s], core_r.at[s], core_s.at[s])
            cb[s][...] += part[s][c]
            if WIDE[s] == 1:
                send(
                    cb[s].at[1 - y_odd], pb[s], pair_s.at[s], pair_r.at[s], y_pair,
                    (("pair", s), pb[s]),
                )
                return
        if WIDE[s] == 1:
            stage -= 1
            if stage == 1:
                arrived(pb[s], pair_r.at[s], pair_s.at[s])
                cb[s][y_odd] += pb[s][...]
            (None, chain_first, chain_second, finish)[stage](s)
        elif stage <= 4:
            long_chain(s, stage)
        else:
            finish(s)

    def by_parity(own, far):
        first = jnp.where(y_odd == 0, own, far)
        second = jnp.where(y_odd == 0, far, own)
        return jnp.concatenate([first, second], axis=0)

    def total(s):
        if s in (G0, W1, G1):
            arrived(yb[s].at[0:3], y_r.at[s], y_s.at[s])
            return by_parity(share[s][0] + yb[s][1], yb[s][0] + yb[s][2])
        if s in (W2, G2):
            arrived(yb[s].at[0:1], y_r.at[s], y_s.at[s])
            return by_parity(share[s][0], yb[s][0])
        return share[s][...].reshape(2 * PIECE[s], RANK)

    def spot(i, steps):
        full, count = (wfull[i], PIECE[GATHERED[i]]) if i < 3 else (ffull.at[i - 3], 16)
        return full.at[c, :, pl.ds(pl.multiple_of(line(steps) * count, count), count)]

    def spots(i, count):
        full, rows = (wfull[i], PIECE[GATHERED[i]]) if i < 3 else (ffull.at[i - 3], 16)
        return full.at[c, :, 0:count * rows]

    def gather_send(i, index, origin, steps):
        ref = spot(i, origin)
        group = (0, 0, 1, 1, 2, 2, 2)[index]
        send(ref, ref, gz_s.at[i], gz_r.at[i, group], z_peer[steps], (("gz", i), spots(i, 7)))

    def gather_wait(i, group):
        arrived(spots(i, (2, 2, 3)[group]), gz_r.at[i, group], gz_s.at[i])

    def gather_core(i, origin):
        ref = spot(i, origin)
        send(ref, ref, gc_s.at[i], gc_r.at[i], partner, (("gc", i), spots(i, 8)))

    def gather_put(i, value):
        spot(i, 0)[...] = value.reshape(2, value.shape[0] // 2, RANK)

    def gather_start(i):
        for index, steps in enumerate((2, -2, 1, -1)):
            gather_send(i, index, 0, steps)
        gather_core(i, 0)

    def gather_step(i):
        gather_wait(i, 0)
        gather_send(i, 4, -2, 2)
        gather_send(i, 5, -2, 1)
        gather_send(i, 6, 2, -1)
        gather_core(i, -2)
        gather_core(i, 2)
        gather_wait(i, 1)
        gather_core(i, -1)
        gather_core(i, 1)

    def gather_last(i):
        gather_wait(i, 2)
        for origin in (-4, -3, 3):
            gather_core(i, origin)

    def gather_end(i):
        arrived(spots(i, 8), gc_r.at[i], gc_s.at[i])

    def w_block(full, l, m):
        return split(full[l - 1][...].reshape(l * RANK, RANK)[m * RANK:(m + 1) * RANK])

    sibling = (x_pair, y_far, y_pair)

    factors = {}

    def pair(own, sibling, upper):
        return jnp.where(
            upper == 0,
            jnp.concatenate([own, sibling], axis=1),
            jnp.concatenate([sibling, own], axis=1),
        )

    def factor(level, paired):
        value = product(split(paired), split(k_matrix(level)), NT)
        factors[level] = split(value)
        gather_put(3 + level, value)
        if level > 0:
            gather_start(3 + level)

    def to_x():
        xs[...] = total(G0)
        for d in range(3):
            send(xs, xb.at[d], x_s.at[0], x_r.at[0], x_peer[d], ("x", xb))

    def level_0():
        arrived(xb, x_r.at[0], x_s.at[0])
        even = x_odd == 0
        own = xs[...] + jnp.where(even, xb[2], xb[0])
        sibling = xb[1] + jnp.where(even, xb[0], xb[2])
        factor(0, pair(own, sibling, x // 2))

    def own_sums(level):
        gather_end(level - 1)
        own = sibs[level - 1]
        for m in range(level):
            own = own - product(factors[m], w_block(wfull, level, m), NN)
        return own

    def sums_of(level):
        sibs[level - 1] = total((G1, G2, G3)[level - 1])

    def exchange(level):
        i = level - 1
        send(sibs.at[i], sib.at[i], sib_s.at[i], sib_r.at[i], sibling[i], (("sib", level), sib.at[i]))

    def level_sums(level):
        sibs[level - 1] = own_sums(level)
        exchange(level)

    def level_factor(level):
        i = level - 1
        arrived(sib.at[i], sib_r.at[i], sib_s.at[i])
        factor(level, pair(sibs[i], sib[i], (x_odd, y // 2, y_odd)[i]))

    block = 256

    def update(level):
        gather_end(3 + level)
        high, low = split(ffull[level].reshape(SIDES, RANK))
        f_hi[...] = high
        f_lo[...] = low
        for i in range(ROWS // block):
            rows = pl.ds(i * block, block)
            solved[rows, :] -= product(
                (u_hi[level, rows, :], u_lo[level, rows, :]), (f_hi[...], f_lo[...]), NT
            )

    def update_half(near):
        core = c if near else 1 - c
        if not near:
            gather_end(6)
        high, low = split(ffull[3, core].reshape(RANK, RANK))
        place = slice(0, RANK) if near else slice(RANK, SIDES)
        f_hi[place, :] = high
        f_lo[place, :] = low
        columns = pl.ds(pl.multiple_of(core * RANK, RANK), RANK)
        for i in range(ROWS // block):
            rows = pl.ds(i * block, block)
            solved[rows, columns] -= product(
                (u_hi[3, rows, :], u_lo[3, rows, :]), (f_hi[place, :], f_lo[place, :]), NT
            )

    def w_start(i):
        gather_put(i, total(GATHERED[i]))
        gather_start(i)

    bind = functools.partial
    def make(s):
        compute(s)
        core_send(s)

    def sc(s, stage):
        return bind(scatter, s, stage)

    def enter():
        pl.semaphore_wait(barrier, len(peers))
        core_send(W1)
        core_send(W2)
        k_start(0)

    order = [
        bind(compute, W1), bind(compute, W2), enter, bind(k_start, 1),
        sc(W1, 1), bind(make, G0), sc(W2, 1),
        bind(make, W3), sc(W1, 2), bind(k_step, 0), sc(G0, 1), sc(W3, 1),
        bind(make, G1), sc(W2, 2), bind(make, G2), bind(k_step, 1), sc(G1, 1), sc(W1, 3),
        bind(make, G3), sc(W3, 2), k_lines_first, sc(G0, 2), sc(G2, 1), sc(W2, 3), sc(W1, 4),
        sc(W3, 3), sc(G0, 3), sc(G1, 2), sc(G3, 1), k_far, k_last, sc(W2, 4), bind(w_start, 0),
        sc(W3, 4), sc(G2, 2), sc(G0, 4), sc(G1, 3), bind(w_start, 1), bind(set_u, 3), sc(G3, 2),
        bind(gather_step, 0), sc(W3, 5), bind(w_start, 2), to_x, sc(G2, 3), sc(G1, 4), sc(G3, 3),
        k_lines_more, bind(gather_last, 0), bind(gather_step, 1), sc(G2, 4), bind(sums_of, 1),
        k_lines_last, k_near, sc(G3, 4),
        level_0, bind(level_sums, 1), bind(gather_step, 2), bind(gather_start, 3), k_middle,
        bind(gather_last, 1), bind(sums_of, 2), sc(G3, 5),
        bind(level_factor, 1), k_pair, bind(level_sums, 2), bind(gather_last, 2),
        bind(gather_step, 3), bind(level_factor, 2), bind(sums_of, 3), bind(level_sums, 3),
        bind(gather_step, 4), bind(gather_last, 3), bind(level_factor, 3),
        bind(gather_step, 5), bind(update, 0), bind(gather_last, 4), bind(gather_step, 6),
        bind(update, 1), bind(gather_last, 5), bind(gather_last, 6), bind(update, 2),
        bind(update_half, True), bind(update_half, False),
    ]
    for step in order:
        step()
    for send_sem, recv_sem, ref in drains.values():
        describe(ref, ref, send_sem, recv_sem, partner).wait_send()


def solve(rhs, u, v, *couples):
    dma = pltpu.SemaphoreType.DMA
    any_space = pl.BlockSpec(memory_space=pl.ANY)
    pairs = []
    for sent, received in (
        ((NS,), (NS,)), ((NS,), (NS,)), ((NS,), (NS, 4)), ((NS,), (NS,)), ((1,), (1,)), ((3,), (3,)),
        ((7,), (7, 3)), ((7,), (7,)), ((2,), (2, 3)), ((4,), (4,)), ((4,), (4,)),
    ):
        pairs += [dma(sent), dma(received)]
    vm = pltpu.VMEM
    scratch = [
        vm((4, ROWS, RANK), F32), vm((4, ROWS, RANK), F32),
        vm((1280, ROWS), BF16), vm((1280, ROWS), BF16),
        vm((4, ROWS, RANK), BF16), vm((4, ROWS, RANK), BF16),
        vm((4, ROWS, RANK), BF16), vm((4, ROWS, RANK), BF16),
    ]
    scratch += [vm((2, 2, q, RANK), F32) for q in QUARTER]
    scratch += [vm((2, q, RANK), F32) for q in QUARTER]
    scratch += [vm((q, RANK), F32) for q in QUARTER]
    scratch += [vm((7, w, h, RANK), F32) for w, h in zip(WIDE, PIECE)]
    scratch += [vm((w, h, RANK), F32) for w, h in zip(WIDE, PIECE)]
    scratch += [vm((3, h, RANK), F32) for h in PIECE]
    scratch += [vm((3, 32, RANK), F32), vm((32, RANK), F32)]
    scratch += [vm((2, 2, QUARTER[s], RANK), F32) for s in GATHERED]
    scratch += [
        vm((4, 2, 2, 128, RANK), F32), vm((SIDES, RANK), BF16), vm((SIDES, RANK), BF16),
        vm((3, 32, RANK), F32), vm((3, 32, RANK), F32),
        vm((2, 64, 128), F32), vm((8, 56, 128), F32),
        vm((8, 8, 2, 8, 128), F32), vm((4, 8, 2, 16, 128), F32),
        vm((2, 8, 2, 32, 128), F32), vm((1, 8, 2, 64, 128), F32),
        vm((4 * RANK, 128), F32),
        dma((9,)),
    ]
    return pl.pallas_call(
        solve_kernel,
        out_shape=pltpu.VMEM((ROWS, SIDES), F32),
        in_specs=[any_space] * 3 + [pl.BlockSpec(memory_space=pltpu.VMEM)] * 4,
        out_specs=pl.BlockSpec(memory_space=pltpu.VMEM),
        scratch_shapes=scratch + pairs,
        compiler_params=pltpu.CompilerParams(
            collective_id=0, has_side_effects=True, vmem_limit_bytes=61 * 1024 * 1024
        ),
        name="solve",
    )(rhs, u, v, *couples)


def solution(mesh):
    placed = (
        P(("rows", "sub"), None),
        P(None, ("rows", "sub"), None),
        P(None, ("rows", "sub"), None),
        P(("rows", "sub"), None),
        P(("rows", "sub"), None),
        P(("rows", "sub"), None),
        P(("rows", "sub"), None),
    )
    return jax.shard_map(
        solve, mesh=mesh, in_specs=placed, out_specs=P(("rows", "sub"), None), check_vma=False
    )
```

```python
import functools

import jax
import jax.numpy as jnp
from jax import lax
from jax.experimental import pallas as pl
from jax.experimental.pallas import tpu as pltpu
from jax.sharding import PartitionSpec as P

F32 = jnp.float32
BF16 = jnp.bfloat16
MESH = pl.DeviceIdType.MESH

RANK = 256
SIDES = 512
ROWS = 1024
STREAMS = (
    (512, 256, 1, True),
    (512, 512, 2, True),
    (0, 512, 0, True),
    (512, 768, 3, False),
    (0, 512, 1, True),
    (0, 512, 2, True),
    (0, 512, 3, False),
)
W1, W2, G0, W3, G1, G2, G3 = range(7)
NS = len(STREAMS)
QUARTER = tuple(rows // 4 for _, rows, _, _ in STREAMS)
PIECE = tuple(rows // 32 for _, rows, _, _ in STREAMS)
WIDE = tuple(1 if paired else 2 for _, _, _, paired in STREAMS)
GATHERED = (W1, W2, W3)
KROWS = (8, 16, 32, 64)
KOFF = (0, 8, 24)


def split(value):
    high = value.astype(BF16)
    return high, (value - high.astype(F32)).astype(BF16)


def product(left, right, dims):
    def one(a, b):
        return lax.dot_general(a, b, (dims, ((), ())), preferred_element_type=F32)

    return one(left[0], right[0]) + (one(left[0], right[1]) + one(left[1], right[0]))


NN = ((1,), (0,))
NT = ((1,), (1,))


def solve_kernel(*refs):
    refs = list(refs)

    def take(count=None):
        if count is None:
            return refs.pop(0)
        return [refs.pop(0) for _ in range(count)]

    rhs_hbm, u_hbm, v_hbm = take(3)
    k_own = take(4)
    solved = take()
    u_in, v_in, a_hi, a_lo, v_hi, v_lo, u_hi, u_lo = take(8)
    part, cb, pb, rz, share, yb = [take(NS) for _ in range(6)]
    xb, xs = take(2)
    wfull = take(3)
    ffull, f_hi, f_lo, sibs, sib = take(5)
    kown, kz, k0, k1, k2, k3, kflat = take(7)
    in_sem = take()
    (core_s, core_r, pair_s, pair_r, z_s, z_r, y_s, y_r, x_s, x_r, sib_s, sib_r,
     gz_s, gz_r, gc_s, gc_r, kz_s, kz_r, kf_s, kf_r, kc_s, kc_r) = take(22)
    assert not refs

    row_index = lax.axis_index("rows")
    sub_index = lax.axis_index("sub")
    x = row_index // 16
    y = row_index // 4 % 4
    z = row_index % 4 * 2 + sub_index // 2
    c = sub_index % 2
    way = 1 - 2 * c

    def line(steps):
        return (z + way * steps + 16) % 8

    def device(x, y, z, c):
        return (x * 16 + y * 4 + z // 2, z % 2 * 2 + c)

    partner = device(x, y, z, 1 - c)
    z_peer = {steps: device(x, y, line(steps), c) for steps in (1, -1, 2, -2)}
    y_peer = [device(x, (y + d) % 4, z, c) for d in (1, 2, 3)]
    x_peer = [device((x + d) % 4, y, z, c) for d in (1, 2, 3)]
    y_odd, x_odd = y % 2, x % 2
    y_pair = device(x, y + 1 - 2 * y_odd, z, c)
    x_pair = device(x + 1 - 2 * x_odd, y, z, c)
    y_far = device(x, 3 - y, z, c)

    def describe(src, dst, s, r, to):
        return pltpu.make_async_remote_copy(
            src_ref=src, dst_ref=dst, send_sem=s, recv_sem=r, device_id=to, device_id_type=MESH
        )

    drains = {}

    def send(src, dst, s, r, to, drain):
        describe(src, dst, s, r, to).start()
        key, ref = drain
        drains[key] = (s, r, ref)

    def arrived(ref, r, s):
        describe(ref, ref, s, r, partner).wait_recv()

    barrier = pltpu.get_barrier_semaphore()
    peers = [partner] + list(z_peer.values()) + y_peer + x_peer
    for peer in peers:
        pl.semaphore_signal(barrier, inc=1, device_id=peer, device_id_type=MESH)

    loads = {}

    def load(name, src, dst, index):
        copy = pltpu.make_async_copy(src, dst, in_sem.at[index])
        copy.start()
        loads[name] = copy

    def load_group(*names):
        for name in names:
            index = ("u0", "v1", "u1", "v2", "rhs", "v0", "u2", "v3", "u3").index(name)
            if name == "rhs":
                load(name, rhs_hbm, solved, index)
            else:
                src, dst = (u_hbm, u_in) if name[0] == "u" else (v_hbm, v_in)
                load(name, src.at[int(name[1])], dst.at[int(name[1])], index)

    load_group("u0", "v1")

    kasm = (k0, k1, k2, k3)
    kline = (x_odd * 4 + y, y, y_odd, 0)

    def k_piece(which, origin):
        return kz.at[origin] if which == 0 else k3.at[0, origin, c]

    def k_send(which, index, origin, steps):
        ref = k_piece(which, origin)
        group = (0, 0, 1, 1, 2, 2, 2)[index]
        every = kz.at[0:7] if which == 0 else k3.at[0, 0:7, c]
        send(ref, ref, kz_s.at[which], kz_r.at[which, group], z_peer[steps], (("kz", which), every))

    def k_wait(which, group):
        count = (2, 2, 3)[group]
        ref = kz.at[0:count] if which == 0 else k3.at[0, 0:count, c]
        arrived(ref, kz_r.at[which, group], kz_s.at[which])

    def k_start(which):
        for level in (0, 1, 2) if which == 0 else (3,):
            count = KROWS[level] // 4
            for b in range(4):
                place = pl.ds(KOFF[level] + b if level < 3 else b, count, stride=4)
                kown[which, place, :] = k_own[level][:, b * 128:(b + 1) * 128]
        if which == 0:
            kz[z] = kown[0, 0:56, :]
        else:
            k3[0, z, c] = kown[1]
        for index, steps in enumerate((2, -2, 1, -1)):
            k_send(which, index, z, steps)

    def k_step(which):
        k_wait(which, 0)
        k_send(which, 4, line(-2), 2)
        k_send(which, 5, line(-2), 1)
        k_send(which, 6, line(2), -1)

    def k_end(which):
        k_wait(which, 1)
        k_wait(which, 2)

    def k_core(level):
        ref = kasm[level].at[:, :, c]
        send(ref, ref, kc_s.at[level], kc_r.at[level], partner, (("kc", level), ref))

    def k_lines_first():
        k_end(0)
        for level in range(3):
            kasm[level][kline[level], :, c] = kz[:, KOFF[level]:KOFF[level] + KROWS[level]]
        for d in range(3):
            send(
                kz.at[:, 0:8], k0.at[kline[0], :, c], kf_s.at[0], kf_r.at[0], y_peer[d],
                ("kf0", k0.at[0:3, :, c]),
            )

    def k_lines_more():
        for d in range(3):
            send(
                kz.at[:, 8:24], k1.at[kline[1], :, c], kf_s.at[1], kf_r.at[1], y_peer[d],
                ("kf1", k1.at[0:3, :, c]),
            )

    def k_lines_last():
        send(
            kz.at[:, 24:56], k2.at[kline[2], :, c], kf_s.at[2], kf_r.at[2], y_pair,
            ("kf2", k2.at[0, :, c]),
        )

    def k_far():
        arrived(k0.at[0:3, :, c], kf_r.at[0], kf_s.at[0])
        ref = k0.at[pl.ds(x_odd * 4, 4), :, c]
        send(ref, ref, kf_s.at[3], kf_r.at[3], x_pair, ("kf3", ref))

    def k_near():
        arrived(k0.at[0:4, :, c], kf_r.at[3], kf_s.at[3])
        k_core(0)

    def k_middle():
        arrived(k1.at[0:3, :, c], kf_r.at[1], kf_s.at[1])
        k_core(1)

    def k_pair():
        arrived(k2.at[0, :, c], kf_r.at[2], kf_s.at[2])
        k_core(2)

    def k_last():
        k_end(1)
        k_core(3)

    def k_matrix(level):
        arrived(kasm[level].at[:, :, c], kc_r.at[level], kc_s.at[level])
        kflat[...] = kasm[level][...].reshape(4 * RANK, 128)
        return jnp.concatenate([kflat[pl.ds(b, RANK, stride=4), :] for b in range(4)], axis=1)

    def set_a(value, first):
        turned = jnp.transpose(value)
        high, low = split(turned)
        a_hi[first:first + value.shape[1], :] = high
        a_lo[first:first + value.shape[1], :] = low

    def set_v(level):
        loads["v%d" % level].wait()
        high, low = split(v_in[level])
        v_hi[level] = high
        v_lo[level] = low

    def set_u(level):
        loads["u%d" % level].wait()
        if level < 3:
            set_a(u_in[level], 512 + RANK * level)
        high, low = split(u_in[level])
        u_hi[level] = high
        u_lo[level] = low

    def compute(s):
        if s == W1:
            set_u(0)
            load_group("u1", "v2", "rhs")
            set_v(1)
        elif s == W2:
            set_u(1)
            load_group("v0", "u2", "v3")
            set_v(2)
        elif s == G0:
            loads["rhs"].wait()
            load_group("u3")
            set_a(solved[...], 0)
            set_v(0)
        elif s == W3:
            set_u(2)
            set_v(3)
        first, rows, level, _ = STREAMS[s]
        for index in range(rows // RANK):
            own = slice(first + index * RANK, first + (index + 1) * RANK)
            value = product((a_hi[own, :], a_lo[own, :]), (v_hi[level], v_lo[level]), NN)
            count = min(QUARTER[s], RANK // 4 if rows != 512 else RANK // 2)
            for at in range(0, RANK, count):
                c_at, rest = divmod(index * RANK + at, 2 * QUARTER[s])
                p_at, row = divmod(rest, QUARTER[s])
                part[s][c_at, p_at, row:row + count, :] = value[at:at + count]

    def core_send(s):
        send(part[s].at[1 - c], cb[s], core_s.at[s], core_r.at[s], partner, (("core", s), cb[s]))

    def piece(s, steps):
        lines = pl.ds(y_odd, 1) if WIDE[s] == 1 else pl.ds(0, 2)
        count = PIECE[s]
        return cb[s].at[lines, pl.ds(pl.multiple_of(line(steps) * count, count), count)]

    def z_send(s, src, index, steps):
        group = 0 if index < 3 else 1
        send(src, rz[s].at[index], z_s.at[s], z_r.at[s, group], z_peer[steps], (("z", s), rz[s]))

    def chain_first(s):
        z_send(s, piece(s, 4), 1, 2)
        z_send(s, piece(s, 3), 0, 1)
        z_send(s, piece(s, -3), 2, -1)
        z_send(s, piece(s, 1), 3, 1)
        z_send(s, piece(s, -1), 4, -1)

    def chain_second(s):
        arrived(rz[s].at[0:3], z_r.at[s, 0], z_s.at[s])
        rz[s][0] = (rz[s][0] + rz[s][1]) + piece(s, 2)[...]
        z_send(s, rz[s].at[0], 5, 2)
        rz[s][2] += piece(s, -2)[...]
        z_send(s, rz[s].at[2], 6, -2)

    def long_chain(s, k):
        if k > 1:
            arrived(rz[s].at[0:2], z_r.at[s, k - 2], z_s.at[s])
            rz[s][k - 2] += piece(s, 5 - k)[...]
        if 1 < k <= 3:
            rz[s][k + 2] += piece(s, k - 4)[...]
        drain = (("z", s), rz[s])
        up = piece(s, 4) if k == 1 else rz[s].at[k - 2]
        send(up, rz[s].at[k - 1], z_s.at[s], z_r.at[s, k - 1], z_peer[1], drain)
        if k <= 3:
            down = piece(s, -3) if k == 1 else rz[s].at[k + 2]
            send(down, rz[s].at[k + 3], z_s.at[s], z_r.at[s, k - 1], z_peer[-1], drain)

    def finish(s):
        if WIDE[s] == 1:
            arrived(rz[s].at[3:7], z_r.at[s, 1], z_s.at[s])
            share[s][...] = piece(s, 0)[...] + ((rz[s][3] + rz[s][4]) + (rz[s][5] + rz[s][6]))
        else:
            arrived(rz[s].at[0:1], z_r.at[s, 3], z_s.at[s])
            share[s][...] = piece(s, 0)[...] + (rz[s][3] + rz[s][6])
        if s in (G0, W1, G1):
            to = y_peer
        elif s in (W2, G2):
            to = [y_pair]
        else:
            to = []
        for d, peer in enumerate(to):
            send(
                share[s], yb[s].at[pl.ds(d, 1)], y_s.at[s], y_r.at[s], peer,
                (("y", s), yb[s].at[0:len(to)]),
            )

    def scatter(s, stage):
        if stage == 1:
            arrived(cb[s], core_r.at[s], core_s.at[s])
            cb[s][...] += part[s][c]
            if WIDE[s] == 1:
                send(
                    cb[s].at[1 - y_odd], pb[s], pair_s.at[s], pair_r.at[s], y_pair,
                    (("pair", s), pb[s]),
                )
                return
        if WIDE[s] == 1:
            stage -= 1
            if stage == 1:
                arrived(pb[s], pair_r.at[s], pair_s.at[s])
                cb[s][y_odd] += pb[s][...]
            (None, chain_first, chain_second, finish)[stage](s)
        elif stage <= 4:
            long_chain(s, stage)
        else:
            finish(s)

    def by_parity(own, far):
        first = jnp.where(y_odd == 0, own, far)
        second = jnp.where(y_odd == 0, far, own)
        return jnp.concatenate([first, second], axis=0)

    def total(s):
        if s in (G0, W1, G1):
            arrived(yb[s].at[0:3], y_r.at[s], y_s.at[s])
            return by_parity(share[s][0] + yb[s][1], yb[s][0] + yb[s][2])
        if s in (W2, G2):
            arrived(yb[s].at[0:1], y_r.at[s], y_s.at[s])
            return by_parity(share[s][0], yb[s][0])
        return share[s][...].reshape(2 * PIECE[s], RANK)

    def spot(i, steps):
        full, count = (wfull[i], PIECE[GATHERED[i]]) if i < 3 else (ffull.at[i - 3], 16)
        return full.at[c, :, pl.ds(pl.multiple_of(line(steps) * count, count), count)]

    def spots(i, count):
        full, rows = (wfull[i], PIECE[GATHERED[i]]) if i < 3 else (ffull.at[i - 3], 16)
        return full.at[c, :, 0:count * rows]

    def gather_send(i, index, origin, steps):
        ref = spot(i, origin)
        group = (0, 0, 1, 1, 2, 2, 2)[index]
        send(ref, ref, gz_s.at[i], gz_r.at[i, group], z_peer[steps], (("gz", i), spots(i, 7)))

    def gather_wait(i, group):
        arrived(spots(i, (2, 2, 3)[group]), gz_r.at[i, group], gz_s.at[i])

    def gather_core(i, origin):
        ref = spot(i, origin)
        send(ref, ref, gc_s.at[i], gc_r.at[i], partner, (("gc", i), spots(i, 8)))

    def gather_put(i, value):
        spot(i, 0)[...] = value.reshape(2, value.shape[0] // 2, RANK)

    def gather_start(i):
        for index, steps in enumerate((2, -2, 1, -1)):
            gather_send(i, index, 0, steps)
        gather_core(i, 0)

    def gather_step(i):
        gather_wait(i, 0)
        gather_send(i, 4, -2, 2)
        gather_send(i, 5, -2, 1)
        gather_send(i, 6, 2, -1)
        gather_core(i, -2)
        gather_core(i, 2)
        gather_wait(i, 1)
        gather_core(i, -1)
        gather_core(i, 1)

    def gather_last(i):
        gather_wait(i, 2)
        for origin in (-4, -3, 3):
            gather_core(i, origin)

    def gather_end(i):
        arrived(spots(i, 8), gc_r.at[i], gc_s.at[i])

    def w_block(full, l, m):
        return split(full[l - 1][...].reshape(l * RANK, RANK)[m * RANK:(m + 1) * RANK])

    sibling = (x_pair, y_far, y_pair)

    factors = {}

    def pair(own, sibling, upper):
        return jnp.where(
            upper == 0,
            jnp.concatenate([own, sibling], axis=1),
            jnp.concatenate([sibling, own], axis=1),
        )

    def factor(level, paired):
        value = product(split(paired), split(k_matrix(level)), NT)
        factors[level] = split(value)
        gather_put(3 + level, value)
        if level > 0:
            gather_start(3 + level)

    def to_x():
        xs[...] = total(G0)
        for d in range(3):
            send(xs, xb.at[d], x_s.at[0], x_r.at[0], x_peer[d], ("x", xb))

    def level_0():
        arrived(xb, x_r.at[0], x_s.at[0])
        even = x_odd == 0
        own = xs[...] + jnp.where(even, xb[2], xb[0])
        sibling = xb[1] + jnp.where(even, xb[0], xb[2])
        factor(0, pair(own, sibling, x // 2))

    def own_sums(level):
        gather_end(level - 1)
        own = sibs[level - 1]
        for m in range(level):
            own = own - product(factors[m], w_block(wfull, level, m), NN)
        return own

    def sums_of(level):
        sibs[level - 1] = total((G1, G2, G3)[level - 1])

    def exchange(level):
        i = level - 1
        send(sibs.at[i], sib.at[i], sib_s.at[i], sib_r.at[i], sibling[i], (("sib", level), sib.at[i]))

    def level_sums(level):
        sibs[level - 1] = own_sums(level)
        exchange(level)

    def level_factor(level):
        i = level - 1
        arrived(sib.at[i], sib_r.at[i], sib_s.at[i])
        factor(level, pair(sibs[i], sib[i], (x_odd, y // 2, y_odd)[i]))

    block = 256

    def update(level):
        gather_end(3 + level)
        high, low = split(ffull[level].reshape(SIDES, RANK))
        f_hi[...] = high
        f_lo[...] = low
        for i in range(ROWS // block):
            rows = pl.ds(i * block, block)
            solved[rows, :] -= product(
                (u_hi[level, rows, :], u_lo[level, rows, :]), (f_hi[...], f_lo[...]), NT
            )

    def update_half(near):
        core = c if near else 1 - c
        if not near:
            gather_end(6)
        high, low = split(ffull[3, core].reshape(RANK, RANK))
        place = slice(0, RANK) if near else slice(RANK, SIDES)
        f_hi[place, :] = high
        f_lo[place, :] = low
        columns = pl.ds(pl.multiple_of(core * RANK, RANK), RANK)
        for i in range(ROWS // block):
            rows = pl.ds(i * block, block)
            solved[rows, columns] -= product(
                (u_hi[3, rows, :], u_lo[3, rows, :]), (f_hi[place, :], f_lo[place, :]), NT
            )

    def w_start(i):
        gather_put(i, total(GATHERED[i]))
        gather_start(i)

    bind = functools.partial
    def make(s):
        compute(s)
        core_send(s)

    def sc(s, stage):
        return bind(scatter, s, stage)

    def enter():
        pl.semaphore_wait(barrier, len(peers))
        core_send(W1)
        core_send(W2)
        k_start(0)

    order = [
        bind(compute, W1), bind(compute, W2), enter, bind(k_start, 1),
        sc(W1, 1), bind(make, G0), sc(W2, 1),
        bind(make, W3), sc(W1, 2), bind(k_step, 0), sc(G0, 1), sc(W3, 1),
        bind(make, G1), sc(W2, 2), bind(make, G2), bind(k_step, 1), sc(G1, 1), sc(W1, 3),
        bind(make, G3), sc(W3, 2), k_lines_first, sc(G0, 2), sc(G2, 1), sc(W2, 3), sc(W1, 4),
        sc(W3, 3), sc(G0, 3), sc(G1, 2), sc(G3, 1), k_far, k_last, sc(W2, 4), bind(w_start, 0),
        sc(W3, 4), sc(G2, 2), sc(G0, 4), sc(G1, 3), bind(w_start, 1), bind(set_u, 3), sc(G3, 2), k_near,
        bind(gather_step, 0), sc(W3, 5), bind(w_start, 2), to_x, sc(G2, 3), sc(G1, 4), sc(G3, 3),
        k_lines_more, bind(gather_last, 0), bind(gather_step, 1), bind(sums_of, 1),
        k_lines_last, level_0, bind(level_sums, 1), sc(G2, 4), sc(G3, 4),
        bind(gather_step, 2), bind(gather_start, 3), k_middle,
        bind(gather_last, 1), bind(sums_of, 2), sc(G3, 5),
        bind(level_factor, 1), k_pair, bind(level_sums, 2), bind(gather_last, 2),
        bind(gather_step, 3), bind(level_factor, 2), bind(sums_of, 3), bind(level_sums, 3),
        bind(gather_step, 4), bind(gather_last, 3), bind(level_factor, 3),
        bind(gather_step, 5), bind(update, 0), bind(gather_last, 4), bind(gather_step, 6),
        bind(update, 1), bind(gather_last, 5), bind(gather_last, 6), bind(update, 2),
        bind(update_half, True), bind(update_half, False),
    ]
    for step in order:
        step()
    for send_sem, recv_sem, ref in drains.values():
        describe(ref, ref, send_sem, recv_sem, partner).wait_send()


def solve(rhs, u, v, *couples):
    dma = pltpu.SemaphoreType.DMA
    any_space = pl.BlockSpec(memory_space=pl.ANY)
    pairs = []
    for sent, received in (
        ((NS,), (NS,)), ((NS,), (NS,)), ((NS,), (NS, 4)), ((NS,), (NS,)), ((1,), (1,)), ((3,), (3,)),
        ((7,), (7, 3)), ((7,), (7,)), ((2,), (2, 3)), ((4,), (4,)), ((4,), (4,)),
    ):
        pairs += [dma(sent), dma(received)]
    vm = pltpu.VMEM
    scratch = [
        vm((4, ROWS, RANK), F32), vm((4, ROWS, RANK), F32),
        vm((1280, ROWS), BF16), vm((1280, ROWS), BF16),
        vm((4, ROWS, RANK), BF16), vm((4, ROWS, RANK), BF16),
        vm((4, ROWS, RANK), BF16), vm((4, ROWS, RANK), BF16),
    ]
    scratch += [vm((2, 2, q, RANK), F32) for q in QUARTER]
    scratch += [vm((2, q, RANK), F32) for q in QUARTER]
    scratch += [vm((q, RANK), F32) for q in QUARTER]
    scratch += [vm((7, w, h, RANK), F32) for w, h in zip(WIDE, PIECE)]
    scratch += [vm((w, h, RANK), F32) for w, h in zip(WIDE, PIECE)]
    scratch += [vm((3, h, RANK), F32) for h in PIECE]
    scratch += [vm((3, 32, RANK), F32), vm((32, RANK), F32)]
    scratch += [vm((2, 2, QUARTER[s], RANK), F32) for s in GATHERED]
    scratch += [
        vm((4, 2, 2, 128, RANK), F32), vm((SIDES, RANK), BF16), vm((SIDES, RANK), BF16),
        vm((3, 32, RANK), F32), vm((3, 32, RANK), F32),
        vm((2, 64, 128), F32), vm((8, 56, 128), F32),
        vm((8, 8, 2, 8, 128), F32), vm((4, 8, 2, 16, 128), F32),
        vm((2, 8, 2, 32, 128), F32), vm((1, 8, 2, 64, 128), F32),
        vm((4 * RANK, 128), F32),
        dma((9,)),
    ]
    return pl.pallas_call(
        solve_kernel,
        out_shape=pltpu.VMEM((ROWS, SIDES), F32),
        in_specs=[any_space] * 3 + [pl.BlockSpec(memory_space=pltpu.VMEM)] * 4,
        out_specs=pl.BlockSpec(memory_space=pltpu.VMEM),
        scratch_shapes=scratch + pairs,
        compiler_params=pltpu.CompilerParams(
            collective_id=0, has_side_effects=True, vmem_limit_bytes=61 * 1024 * 1024
        ),
        name="solve",
    )(rhs, u, v, *couples)


def solution(mesh):
    placed = (
        P(("rows", "sub"), None),
        P(None, ("rows", "sub"), None),
        P(None, ("rows", "sub"), None),
        P(("rows", "sub"), None),
        P(("rows", "sub"), None),
        P(("rows", "sub"), None),
        P(("rows", "sub"), None),
    )
    return jax.shard_map(
        solve, mesh=mesh, in_specs=placed, out_specs=P(("rows", "sub"), None), check_vma=False
    )
```
